512 devices in a mesh: cell: 32 (over z, y_lo), gene: 16 (over x, y_hi, core).
Axes of the slice: x: 4, y: 4 (y_hi: 2, y_lo: 2; y = y_hi * 2 + y_lo), z: 16, core: 2. Of those that a mesh axis runs over, the one named last changes fastest.
Arguments:
- counts: int32 [32768, 16384], P('cell', 'gene'), may hold values from 0 to 4
- factors: float32 [32768, 64], P(('cell', 'gene')), may hold values from -1.5 to 1.5
- loadings: float32 [16384, 64], P(('gene', 'cell')), may hold values from -1.5 to 1.5
- cell_offset: float32 [32768], P('cell'), may hold values from -1.2 to 1.2
- gene_offset: float32 [16384], P('gene'), may hold values from -1.2 to 1.2
Outputs:
- new_factors: float32 [32768, 64], P(('cell', 'gene'))
- new_loadings: float32 [16384, 64], P(('gene', 'cell'))
The draws below stay inside these ranges and needn't reach their ends.
All inputs are finite; a program needn't handle non-finite values.
Results may differ from the reference program's by a relative error of at most 0.0003.
Values sent between devices are 32-bit elements; how exact they have to be, the bound alone decides.
A program may use at most 64 MiB of HBM per device.

```python
import jax
import jax.numpy as jnp
from jax import lax

K = 64
G = 16384
CELL_DEV = 1024
ITERS = 2
C = 32768
N_CELL = 32


def touch_ends(drawn, rng, low, high):
    dims = drawn.shape
    spot = [jax.random.randint(jax.random.fold_in(rng, axis), (), 0, dims[axis]) for axis in range(len(dims))]
    drawn = drawn.at[tuple(spot)].set(low)
    longest = dims.index(max(dims))
    spot[longest] = (spot[longest] + 1) % dims[longest]
    return drawn.at[tuple(spot)].set(high)


def block_scale(stream_key, extent, shards, low, high):
    factor_of, own = 1.0, jax.random.fold_in(stream_key, 6)
    for axis_at, shards_of in shards:
        heights = jnp.exp(jax.random.uniform(jax.random.fold_in(own, axis_at), (shards_of,), jnp.float32, low / len(shards), high / len(shards)))
        factor_of = factor_of * jnp.repeat(heights, extent[axis_at] // shards_of).reshape([-1 if axis == axis_at else 1 for axis in range(len(extent))])
    return factor_of


def bell_draw(rng, shape, spread, bound, shards=(), held_as=jnp.bfloat16):
    level = block_scale(rng, shape, shards, -0.22, 0.18) if shards else 1.0
    result = jax.random.normal(rng, shape, jnp.float32) * spread * level
    return jnp.minimum(jnp.maximum(result, -bound), bound).astype(held_as)


def setup_inputs(seed: int = 0) -> dict:
    key_list = jax.random.split(jax.random.key(seed), 6)
    counts = touch_ends(jax.random.randint(key_list[0], (C, G), 0, 5), jax.random.fold_in(key_list[0], 1), 0, 4).astype(jnp.int32)
    factors = bell_draw(key_list[1], (C, K), 0.25, 1.5, ((0, 512),), jnp.float32)
    loadings = bell_draw(key_list[2], (G, K), 0.25, 1.5, ((0, 512),), jnp.float32)
    cell_offset = jnp.clip(jax.random.uniform(key_list[3], (C,), jnp.float32, -1.2, 1.2) * block_scale(key_list[3], (C,), ((0, 32),), -0.4, 0.0), -1.2, 1.2)
    gene_offset = jnp.clip(jax.random.uniform(key_list[4], (G,), jnp.float32, -1.2, 1.2) * block_scale(key_list[4], (G,), ((0, 16),), -0.4, 0.0), -1.2, 1.2)
    return dict(counts=counts, factors=factors, loadings=loadings, cell_offset=cell_offset, gene_offset=gene_offset)


epsilon = 1e-6
step_cap = 0.25


def bounded(ratio):
    return step_cap * jnp.tanh(ratio / step_cap)


def predict(factor_rows, loading_rows, cell_part, gene_part, count_part):
    linear = jnp.dot(factor_rows, loading_rows.T, preferred_element_type=jnp.float32, precision=lax.Precision.HIGHEST)
    linear = linear + cell_part[:, None] + gene_part[None, :]
    means = jnp.exp(linear)
    excess = means - count_part.astype(jnp.float32)
    return means, excess


def reference(counts, factors, loadings, cell_offset, gene_offset):
    count_blocks = counts.reshape(N_CELL, CELL_DEV, G)
    offset_blocks = cell_offset.reshape(N_CELL, CELL_DEV)
    current_u = factors
    current_v = loadings
    for iteration in range(ITERS):
        factor_blocks = current_u.reshape(N_CELL, CELL_DEV, K)
        squared_v = current_v * current_v

        def factor_step(items):
            count_part, factor_rows, cell_part = items
            means, excess = predict(factor_rows, current_v, cell_part, gene_offset, count_part)
            grad_u = jnp.dot(excess, current_v, preferred_element_type=jnp.float32, precision=lax.Precision.HIGHEST)
            curv_u = jnp.dot(means, squared_v, preferred_element_type=jnp.float32, precision=lax.Precision.HIGHEST)
            return factor_rows - bounded(grad_u / (curv_u + epsilon))

        new_blocks = lax.map(factor_step, (count_blocks, factor_blocks, offset_blocks))
        current_u = new_blocks.reshape(C, K)

        def loading_sum(carry, items):
            count_part, factor_rows, cell_part = items
            means, excess = predict(factor_rows, current_v, cell_part, gene_offset, count_part)
            grad_v = jnp.dot(excess.T, factor_rows, preferred_element_type=jnp.float32, precision=lax.Precision.HIGHEST)
            curv_v = jnp.dot(means.T, factor_rows * factor_rows, preferred_element_type=jnp.float32, precision=lax.Precision.HIGHEST)
            return (carry[0] + grad_v, carry[1] + curv_v), None

        start = (jnp.zeros((G, K), jnp.float32), jnp.zeros((G, K), jnp.float32))
        totals, unused = lax.scan(loading_sum, start, (count_blocks, new_blocks, offset_blocks))
        current_v = current_v - bounded(totals[0] / (totals[1] + epsilon))
    return current_u, current_v
```

```python
import functools

import jax
import jax.numpy as jnp
from jax import lax
from jax.experimental import pallas as pl
from jax.experimental.pallas import tpu as pltpu
from jax.sharding import PartitionSpec as P

ITERS = 2
EPSILON = 1e-06
STEP_CAP = 0.25
LOG2E = 1.4426950408889634
F32, BF16 = jnp.float32, jnp.bfloat16
MESH = pl.DeviceIdType.MESH

ZG, ZL, YL = 4, 4, 2
X, YH, CO = 4, 2, 2
RANK = 64
UROWS, VROWS = 64, 32
CELLS = X * YH * CO * UROWS
GENES = ZG * ZL * YL * VROWS
UCHUNK = YH * CO * UROWS
VCHUNK = ZL * YL * VROWS
FAR_FIRST = (2, 1, 3, 0)
U_CORE = 0
U_CHIP = U_CORE + X
V_PAIR = U_CHIP + X * YH
V_LINE = V_PAIR + ZG
V_RING = V_LINE + ZG * ZL
GU_CHIP = V_RING + ZG
GU_CORE = GU_CHIP + X * YH
GV_RING = GU_CORE + X * YH
GV_LINE = GV_RING + ZG
GV_PAIR = GV_LINE + ZG * ZL
SLOTS = GV_PAIR + ZG


def split(x):
    high = x.astype(BF16).astype(F32)
    return high, x - high


def left_half(shape):
    return lax.broadcasted_iota(jnp.int32, shape, len(shape) - 1) < RANK


def swap(x):
    return pltpu.roll(x, RANK, axis=x.ndim - 1)


def pairs(left, right):
    mask = left_half(left.shape)
    first = jnp.where(mask, left, swap(right))
    second = jnp.where(mask, swap(left), right)
    return first, second


def unpack_to(ref, column, block, left, right):
    first, second = pairs(left, right)
    n = first.shape[-2]
    ref[pl.ds(block, n), pl.ds(column, 128)] = first.astype(BF16)
    ref[pl.ds(block + n, n), pl.ds(column, 128)] = second.astype(BF16)


def far_first(j):
    return (2 + 3 * j - (j * (j - 1)) // 2) % 4


def kernel(
    counts_hbm, u_ref, v_ref, cell_ref, gene_ref, new_u, new_v,
    cnt32, cnt, cnt_t, u_eta, u_sum, v_eta, v_sum, cell_cols, gene_cols,
    own_u, own_v, ubuf, vbuf, part_u, core_in, sum_u, chip_in,
    part_v, pair_in, sum1, line_in, sum2, ring_in, load_sem, send_sem, recv_sem,
):
    c, g = lax.axis_index("cell"), lax.axis_index("gene")
    z, yl = c // YL, c % YL
    zg, zl = z // ZL, z % ZL
    chip, co = g // CO, g % CO
    x, yh = chip // YH, chip % YH

    def cell_dev(dg, dl, dy):
        there = ((zg + dg) % ZG) * ZL + (zl + dl) % ZL
        return (there * YL + (yl + dy) % YL, g)

    def gene_dev(dx, dh, dc):
        there = ((x + dx) % X) * YH + (yh + dh) % YH
        return (c, there * CO + (co + dc) % CO)

    chips = [(dx, dh) for dx in FAR_FIRST for dh in (1, 0) if dx or dh]
    peers = [gene_dev(dx, dh, 0) for dx, dh in chips] + [gene_dev(0, 0, 1)]
    peers += [cell_dev(d, 0, 0) for d in (2, 1, 3)]
    peers += [cell_dev(0, d, 0) for d in (1, 2, 3)] + [cell_dev(0, 0, 1)]
    barrier = pltpu.get_barrier_semaphore()
    for peer in peers:
        pl.semaphore_signal(barrier, inc=1, device_id=peer, device_id_type=MESH)

    def load(k):
        rows = pl.ds(k * 256, 256)
        return pltpu.make_async_copy(counts_hbm.at[rows], cnt32.at[rows], load_sem.at[k])

    for k in range(CELLS // 256):
        load(k).start()

    started = []

    def send(era, slot, src, dst, device):
        copy = pltpu.make_async_remote_copy(
            src_ref=src, dst_ref=dst, send_sem=send_sem.at[era, slot],
            recv_sem=recv_sem.at[era, slot], device_id=device, device_id_type=MESH,
        )
        copy.start()

    def sent(era, slot, src, dst, device):
        send(era, slot, src, dst, device)
        started.append((era, slot, src))

    def arrived(era, slot, ref):
        pltpu.make_async_remote_copy(
            src_ref=ref, dst_ref=ref, send_sem=send_sem.at[era, slot],
            recv_sem=recv_sem.at[era, slot], device_id=(c, g), device_id_type=MESH,
        ).wait_recv()

    def pack(rows):
        half = rows.shape[0] // 2
        return jnp.where(left_half((half, 128)), rows[:half], swap(rows[half:]))

    own_u[...] = jnp.zeros_like(own_u)
    own_v[...] = jnp.zeros_like(own_v)
    own_u[:, :RANK] = u_ref[...]
    own_v[:, :RANK] = v_ref[...]

    def offset_columns(row, first_offset, first_one, out):
        high, rest = split(row)
        mid, low = split(rest)
        index = lax.broadcasted_iota(jnp.int32, (128, row.shape[1]), 0)
        rows = jnp.zeros((128, row.shape[1]), F32)
        for k, part in enumerate((high, mid, low)):
            rows = jnp.where(index == first_offset + k, part, rows)
            rows = jnp.where(index == first_one + k, 1.0, rows)
        out[...] = rows.T

    ubuf[0, chip, co] = pack(own_u[...])
    vbuf[0, zg, zl, yl] = pack(own_v[...])
    pl.semaphore_wait(barrier, len(peers))

    def gather_u_start(era):
        mine = ubuf.at[era, chip, co]
        for dx, dh in chips:
            sent(era, GU_CHIP + dx * YH + dh, mine, mine, gene_dev(dx, dh, 0))
        sent(era, GU_CORE, mine, mine, gene_dev(0, 0, 1))

    def gather_u_finish(era):
        order = [(1, 0), (3, 0), (0, 1), (2, 0), (1, 1), (3, 1), (2, 1)]
        for dx, dh in order:
            block = ubuf.at[era, ((x - dx) % X) * YH + (yh - dh) % YH, co]
            arrived(era, GU_CHIP + dx * YH + dh, block)
            sent(era, GU_CORE + dx * YH + dh, block, block, gene_dev(0, 0, 1))
        for dx, dh in [(0, 0)] + order:
            block = ubuf.at[era, ((x - dx) % X) * YH + (yh - dh) % YH, 1 - co]
            arrived(era, GU_CORE + dx * YH + dh, block)

    def v_line(era, e):
        block = vbuf.at[era, (zg - e) % ZG, zl, yl]
        for d in (3, 2, 1):
            sent(era, GV_LINE + e * ZL + d, block, block, cell_dev(0, d, 0))

    def v_pair(era, e):
        for d in (1, 2, 3):
            arrived(era, GV_LINE + e * ZL + d, vbuf.at[era, (zg - e) % ZG, (zl - d) % ZL, yl])
        blocks = vbuf.at[era, (zg - e) % ZG, :, yl]
        sent(era, GV_PAIR + e, blocks, blocks, cell_dev(0, 0, 1))

    def v_ring(era, e):
        arrived(era, GV_RING + e, vbuf.at[era, (zg - e) % ZG, zl, yl])
        v_line(era, e)

    def gather_v_start(era):
        mine = vbuf.at[era, zg, zl, yl]
        for d in (2, 1, 3):
            sent(era, GV_RING + d, mine, mine, cell_dev(d, 0, 0))
        v_line(era, 0)

    def gather_v_finish(era):
        v_pair(era, 0)
        v_ring(era, 1)
        v_ring(era, 3)
        v_pair(era, 1)
        v_pair(era, 3)
        v_ring(era, 2)
        v_pair(era, 2)
        for e in (0, 1, 3, 2):
            arrived(era, GV_PAIR + e, vbuf.at[era, (zg - e) % ZG, :, 1 - yl])

    def assemble(packed, rows, eta, total, columns, scale):
        plain_h, plain_l = split(packed)
        square_h, square_l = split(packed * packed)
        n = rows // 2

        def put(ref, column, left, right):
            first, second = pairs(left, right)
            both = jnp.concatenate([first.astype(BF16), second.astype(BF16)], axis=1)
            ref[:, column:column + 128] = both.reshape(ref.shape[0], 128)

        put(total, 0, plain_h, square_h)
        put(total, 128, plain_l, square_l)
        mask = left_half(columns.shape)
        if scale:
            high, low = split(packed * LOG2E)
            put(eta, 0, high, low)
            third = high
        else:
            put(eta, 0, plain_h, plain_h)
            third = plain_l
        first, second = pairs(third, third)
        both = jnp.concatenate([first, second], axis=1).reshape(eta.shape[0], 128)
        eta[:, 128:] = jnp.where(mask, both, columns[...]).astype(BF16)

    def assemble_u(era):
        assemble(ubuf[era].reshape(X * YH * CO, UROWS // 2, 128), UROWS, u_eta, u_sum, cell_cols, True)

    def assemble_v(era):
        assemble(vbuf[era].reshape(ZG * ZL * YL, VROWS // 2, 128), VROWS, v_eta, v_sum, gene_cols, False)

    def sums(row_eta, column_eta, weights, count_ref, first, rows):
        here = pl.ds(pl.multiple_of(first, rows), rows)
        eta = lax.dot_general(
            row_eta[here, :], column_eta[...], (((1,), (1,)), ((), ())), preferred_element_type=F32
        )
        means = jnp.exp2(eta)
        high = means.astype(BF16)
        low = (means - high.astype(F32)).astype(BF16)
        w = weights[...]
        acc = jnp.dot(high, w, preferred_element_type=F32) + jnp.dot(low, w, preferred_element_type=F32)
        seen = jnp.dot(count_ref[here, :], w, preferred_element_type=F32)
        total = acc[:, :128] + acc[:, 128:]
        seen = seen[:, :128] + seen[:, 128:]
        return total - jnp.where(left_half(seen.shape), seen, 0.0)

    def updated(own, total):
        return own - STEP_CAP * jnp.tanh((total / (swap(total) + EPSILON)) / STEP_CAP)

    def factor_step(it):
        def chunk(j, carry):
            there = (x + far_first(j)) % X
            out = sums(u_eta, v_eta, v_sum, cnt, there * UCHUNK, UCHUNK)
            part_u[it, there] = out.reshape(YH, CO, UROWS, 128)
            send(it, U_CORE + j, part_u.at[it, there, :, 1 - co], core_in.at[it, j], gene_dev(0, 0, 1))
            return carry

        lax.fori_loop(0, X, chunk, 0)
        for j, dx in enumerate(FAR_FIRST):
            there = (x + dx) % X
            started.append((it, U_CORE + j, core_in.at[it, j]))
            arrived(it, U_CORE + j, core_in.at[it, j])
            sum_u[it, j] = part_u[it, there, :, co] + core_in[it, j]
            for dh in (1, 0):
                if dx or dh:
                    slot = dx * YH + dh
                    sent(it, U_CHIP + slot, sum_u.at[it, j, (yh + dh) % YH], chip_in.at[it, slot], gene_dev(dx, dh, 0))
        total = sum_u[it, len(FAR_FIRST) - 1, yh]
        for dx, dh in [(1, 0), (3, 0), (0, 1), (2, 0), (1, 1), (3, 1), (2, 1)]:
            slot = dx * YH + dh
            arrived(it, U_CHIP + slot, chip_in.at[it, slot])
            total = total + chip_in[it, slot]
        own_u[...] = updated(own_u[...], total)

    def loading_step(it):
        def chunk(j, carry):
            there = (zg + far_first(j)) % ZG
            out = sums(v_eta, u_eta, u_sum, cnt_t, there * VCHUNK, VCHUNK)
            part_v[it, there] = out.reshape(ZL, YL, VROWS, 128)
            send(it, V_PAIR + j, part_v.at[it, there, :, 1 - yl], pair_in.at[it, j], cell_dev(0, 0, 1))
            return carry

        lax.fori_loop(0, ZG, chunk, 0)
        for j, dg in enumerate(FAR_FIRST):
            there = (zg + dg) % ZG
            started.append((it, V_PAIR + j, pair_in.at[it, j]))
            arrived(it, V_PAIR + j, pair_in.at[it, j])
            sum1[it, j] = part_v[it, there, :, yl] + pair_in[it, j]
            for d in (3, 2, 1):
                sent(it, V_LINE + j * ZL + d, sum1.at[it, j, (zl + d) % ZL], line_in.at[it, j, d], cell_dev(0, d, 0))
        for j, dg in enumerate(FAR_FIRST):
            total = sum1[it, j, zl]
            for d in (1, 2, 3):
                arrived(it, V_LINE + j * ZL + d, line_in.at[it, j, d])
                total = total + line_in[it, j, d]
            if dg:
                sum2[it, j] = total
                sent(it, V_RING + dg, sum2.at[it, j], ring_in.at[it, dg], cell_dev(dg, 0, 0))
        for dg in (1, 3, 2):
            arrived(it, V_RING + dg, ring_in.at[it, dg])
            total = total + ring_in[it, dg]
        own_v[...] = updated(own_v[...], total)

    gather_v_start(0)
    gather_u_start(0)
    offset_columns(cell_ref[...] * LOG2E, RANK, RANK + 3, cell_cols)
    offset_columns(gene_ref[...] * LOG2E, RANK + 3, RANK, gene_cols)

    def prepare(k, carry):
        load(k).wait()
        rows = pl.ds(pl.multiple_of(k * 256, 256), 256)
        block = cnt32[rows, :].astype(F32)
        cnt[rows, :] = block.astype(BF16)
        cnt_t[:, rows] = block.T.astype(BF16)
        return carry

    gather_u_finish(0)
    lax.fori_loop(0, CELLS // 256, prepare, 0)
    gather_v_finish(0)
    assemble_u(0)
    assemble_v(0)
    for it in range(ITERS):
        factor_step(it)
        ubuf[it + 1, chip, co] = pack(own_u[...])
        if it + 1 == ITERS:
            new_u[...] = own_u[:, :RANK]
        gather_u_start(it + 1)
        gather_u_finish(it + 1)
        assemble_u(it + 1)
        loading_step(it)
        if it + 1 < ITERS:
            vbuf[it + 1, zg, zl, yl] = pack(own_v[...])
            gather_v_start(it + 1)
            gather_v_finish(it + 1)
            assemble_v(it + 1)
    new_v[...] = own_v[:, :RANK]
    for era, slot, src in started:
        pltpu.make_async_remote_copy(
            src_ref=src, dst_ref=src, send_sem=send_sem.at[era, slot],
            recv_sem=recv_sem.at[era, slot], device_id=(c, g), device_id_type=MESH,
        ).wait_send()


def per_device(counts, factors, loadings, cell_offset, gene_offset):
    vmem = pl.BlockSpec(memory_space=pltpu.VMEM)
    scratch = [
        pltpu.VMEM((CELLS, GENES), jnp.int32),
        pltpu.VMEM((CELLS, GENES), BF16),
        pltpu.VMEM((GENES, CELLS), BF16),
        pltpu.VMEM((CELLS, 256), BF16),
        pltpu.VMEM((CELLS, 256), BF16),
        pltpu.VMEM((GENES, 256), BF16),
        pltpu.VMEM((GENES, 256), BF16),
        pltpu.VMEM((CELLS, 128), F32),
        pltpu.VMEM((GENES, 128), F32),
        pltpu.VMEM((UROWS, 128), F32),
        pltpu.VMEM((VROWS, 128), F32),
        pltpu.VMEM((ITERS + 1, X * YH, CO, UROWS // 2, 128), F32),
        pltpu.VMEM((ITERS, ZG, ZL, YL, VROWS // 2, 128), F32),
        pltpu.VMEM((ITERS, X, YH, CO, UROWS, 128), F32),
        pltpu.VMEM((ITERS, X, YH, UROWS, 128), F32),
        pltpu.VMEM((ITERS, X, YH, UROWS, 128), F32),
        pltpu.VMEM((ITERS, X * YH, UROWS, 128), F32),
        pltpu.VMEM((ITERS, ZG, ZL, YL, VROWS, 128), F32),
        pltpu.VMEM((ITERS, ZG, ZL, VROWS, 128), F32),
        pltpu.VMEM((ITERS, ZG, ZL, VROWS, 128), F32),
        pltpu.VMEM((ITERS, ZG, ZL, VROWS, 128), F32),
        pltpu.VMEM((ITERS, ZG, VROWS, 128), F32),
        pltpu.VMEM((ITERS, ZG, VROWS, 128), F32),
        pltpu.SemaphoreType.DMA((CELLS // 256,)),
        pltpu.SemaphoreType.DMA((ITERS + 1, SLOTS)),
        pltpu.SemaphoreType.DMA((ITERS + 1, SLOTS)),
    ]
    return pl.pallas_call(
        kernel,
        name="sweeps",
        out_shape=(
            jax.ShapeDtypeStruct((UROWS, RANK), F32),
            jax.ShapeDtypeStruct((VROWS, RANK), F32),
        ),
        in_specs=[pl.BlockSpec(memory_space=pl.ANY), vmem, vmem, vmem, vmem],
        out_specs=(vmem, vmem),
        scratch_shapes=scratch,
        compiler_params=pltpu.CompilerParams(
            collective_id=0, has_side_effects=True, vmem_limit_bytes=48 * 1024 * 1024
        ),
    )(counts, factors, loadings, cell_offset.reshape(1, -1), gene_offset.reshape(1, -1))


def solution(mesh):
    in_specs = (
        P("cell", "gene"),
        P(("cell", "gene"), None),
        P(("gene", "cell"), None),
        P("cell"),
        P("gene"),
    )
    out_specs = (P(("cell", "gene"), None), P(("gene", "cell"), None))
    return jax.shard_map(
        per_device, mesh=mesh, in_specs=in_specs, out_specs=out_specs, check_vma=False
    )
```

```python
import functools

import jax
import jax.numpy as jnp
from jax import lax
from jax.experimental import pallas as pl
from jax.experimental.pallas import tpu as pltpu
from jax.sharding import PartitionSpec as P

ITERS = 2
EPSILON = 1e-06
STEP_CAP = 0.25
LOG2E = 1.4426950408889634
F32, BF16 = jnp.float32, jnp.bfloat16
MESH = pl.DeviceIdType.MESH

ZG, ZL, YL = 4, 4, 2
Z = ZG * ZL
X, YH, CO = 4, 2, 2
RANK = 64
UROWS, VROWS = 64, 32
CELLS = X * YH * CO * UROWS
GENES = ZG * ZL * YL * VROWS
UCHUNK = YH * CO * UROWS
VCHUNK = ZL * YL * VROWS
FAR_FIRST = (2, 1, 3, 0)
U_CORE = 0
U_CHIP = U_CORE + X
V_PAIR = U_CHIP + X * YH
V_LINE = V_PAIR + ZG
V_RING = V_LINE + ZG * ZL
GU_CHIP = V_RING + ZG
GU_CORE = GU_CHIP + X * YH
GV_Z = GU_CORE + X * YH
GV_PAIR = GV_Z + ZG * ZL
SLOTS = GV_PAIR + ZG * ZL


def split(x):
    high = x.astype(BF16).astype(F32)
    return high, x - high


def left_half(shape):
    return lax.broadcasted_iota(jnp.int32, shape, len(shape) - 1) < RANK


def swap(x):
    return pltpu.roll(x, RANK, axis=x.ndim - 1)


def pairs(left, right):
    mask = left_half(left.shape)
    first = jnp.where(mask, left, swap(right))
    second = jnp.where(mask, swap(left), right)
    return first, second


def unpack_to(ref, column, block, left, right):
    first, second = pairs(left, right)
    n = first.shape[-2]
    ref[pl.ds(block, n), pl.ds(column, 128)] = first.astype(BF16)
    ref[pl.ds(block + n, n), pl.ds(column, 128)] = second.astype(BF16)


def far_first(j):
    return (2 + 3 * j - (j * (j - 1)) // 2) % 4


def kernel(
    counts_hbm, u_hbm, v_hbm, cell_hbm, gene_hbm, new_rows,
    u_ref, v_ref, cell_ref, gene_ref, cnt32, cnt, cnt_t, u_eta, u_sum, v_eta, v_sum, cell_cols, gene_cols,
    own_u, own_v, ubuf, vbuf, part_u, core_in, sum_u, chip_in,
    part_v, pair_in, sum1, line_in, sum2, ring_in, load_sem, send_sem, recv_sem,
):
    c, g = lax.axis_index("cell"), lax.axis_index("gene")
    z, yl = c // YL, c % YL
    zg, zl = z // ZL, z % ZL
    chip, co = g // CO, g % CO
    x, yh = chip // YH, chip % YH

    def cell_dev(dg, dl, dy):
        there = ((zg + dg) % ZG) * ZL + (zl + dl) % ZL
        return (there * YL + (yl + dy) % YL, g)

    def gene_dev(dx, dh, dc):
        there = ((x + dx) % X) * YH + (yh + dh) % YH
        return (c, there * CO + (co + dc) % CO)

    def z_dev(d):
        return (((z + d) % Z) * YL + yl, g)

    far = [d for k in range(Z // 2, 0, -1) for d in dict.fromkeys((k, Z - k))]
    chips = [(dx, dh) for dx in FAR_FIRST for dh in (1, 0) if dx or dh]
    peers = [z_dev(d) for d in far] + [gene_dev(dx, dh, 0) for dx, dh in chips]
    peers += [cell_dev(0, 0, 1), gene_dev(0, 0, 1)]
    barrier = pltpu.get_barrier_semaphore()
    for peer in peers:
        pl.semaphore_signal(barrier, inc=1, device_id=peer, device_id_type=MESH)

    def load(k):
        rows = pl.ds(k * 256, 256)
        return pltpu.make_async_copy(counts_hbm.at[rows], cnt32.at[rows], load_sem.at[k])

    small = [
        pltpu.make_async_copy(src, dst, load_sem.at[CELLS // 256 + k])
        for k, (src, dst) in enumerate(
            ((v_hbm, v_ref), (u_hbm, u_ref), (cell_hbm, cell_ref), (gene_hbm, gene_ref))
        )
    ]
    for copy in small:
        copy.start()
    for k in range(CELLS // 256):
        load(k).start()

    started = []

    def send(era, slot, src, dst, device):
        copy = pltpu.make_async_remote_copy(
            src_ref=src, dst_ref=dst, send_sem=send_sem.at[era, slot],
            recv_sem=recv_sem.at[era, slot], device_id=device, device_id_type=MESH,
        )
        copy.start()

    def sent(era, slot, src, dst, device):
        send(era, slot, src, dst, device)
        started.append((era, slot, src))

    def arrived(era, slot, ref):
        pltpu.make_async_remote_copy(
            src_ref=ref, dst_ref=ref, send_sem=send_sem.at[era, slot],
            recv_sem=recv_sem.at[era, slot], device_id=(c, g), device_id_type=MESH,
        ).wait_recv()

    def pack(rows):
        half = rows.shape[0] // 2
        return jnp.where(left_half((half, 128)), rows[:half], swap(rows[half:]))

    own_u[...] = jnp.zeros_like(own_u)
    own_v[...] = jnp.zeros_like(own_v)
    for copy in small:
        copy.wait()
    own_u[:, :RANK] = u_ref[...]
    own_v[:, :RANK] = v_ref[...]

    def offset_columns(row, first_offset, first_one, out):
        high, rest = split(row)
        mid, low = split(rest)
        index = lax.broadcasted_iota(jnp.int32, (128, row.shape[1]), 0)
        rows = jnp.zeros((128, row.shape[1]), F32)
        for k, part in enumerate((high, mid, low)):
            rows = jnp.where(index == first_offset + k, part, rows)
            rows = jnp.where(index == first_one + k, 1.0, rows)
        out[...] = rows.T

    ubuf[0, chip, co] = pack(own_u[...])
    vbuf[0, z, yl] = pack(own_v[...])
    pl.semaphore_wait(barrier, len(peers))

    def gather_u_start(era):
        mine = ubuf.at[era, chip, co]
        for dx, dh in chips:
            sent(era, GU_CHIP + dx * YH + dh, mine, mine, gene_dev(dx, dh, 0))
        sent(era, GU_CORE, mine, mine, gene_dev(0, 0, 1))

    def gather_u_finish(era):
        order = [(1, 0), (3, 0), (0, 1), (2, 0), (1, 1), (3, 1), (2, 1)]
        for dx, dh in order:
            block = ubuf.at[era, ((x - dx) % X) * YH + (yh - dh) % YH, co]
            arrived(era, GU_CHIP + dx * YH + dh, block)
            sent(era, GU_CORE + dx * YH + dh, block, block, gene_dev(0, 0, 1))
        for dx, dh in [(0, 0)] + order:
            block = ubuf.at[era, ((x - dx) % X) * YH + (yh - dh) % YH, 1 - co]
            arrived(era, GU_CORE + dx * YH + dh, block)

    def gather_v_start(era):
        mine = vbuf.at[era, z, yl]
        for d in far:
            sent(era, GV_Z + d, mine, mine, z_dev(d))
        sent(era, GV_PAIR, mine, mine, cell_dev(0, 0, 1))

    def gather_v_finish(era):
        near = [d for d in reversed(far)]
        for d in near:
            block = vbuf.at[era, (z - d) % Z, yl]
            arrived(era, GV_Z + d, block)
            sent(era, GV_PAIR + d, block, block, cell_dev(0, 0, 1))
        for d in [0] + near:
            arrived(era, GV_PAIR + d, vbuf.at[era, (z - d) % Z, 1 - yl])

    def assemble(packed, rows, eta, total, columns, scale):
        plain_h, plain_l = split(packed)
        square_h, square_l = split(packed * packed)
        n = rows // 2

        def put(ref, column, left, right):
            first, second = pairs(left, right)
            both = jnp.concatenate([first.astype(BF16), second.astype(BF16)], axis=1)
            ref[:, column:column + 128] = both.reshape(ref.shape[0], 128)

        put(total, 0, plain_h, square_h)
        put(total, 128, plain_l, square_l)
        mask = left_half(columns.shape)
        if scale:
            high, low = split(packed * LOG2E)
            put(eta, 0, high, low)
            third = high
        else:
            put(eta, 0, plain_h, plain_h)
            third = plain_l
        first, second = pairs(third, third)
        both = jnp.concatenate([first, second], axis=1).reshape(eta.shape[0], 128)
        eta[:, 128:] = jnp.where(mask, both, columns[...]).astype(BF16)

    def assemble_u(era):
        assemble(ubuf[era].reshape(X * YH * CO, UROWS // 2, 128), UROWS, u_eta, u_sum, cell_cols, True)

    def assemble_v(era):
        assemble(vbuf[era].reshape(ZG * ZL * YL, VROWS // 2, 128), VROWS, v_eta, v_sum, gene_cols, False)

    def sums(row_eta, column_eta, weights, count_ref, first, rows):
        here = pl.ds(pl.multiple_of(first, rows), rows)
        eta = lax.dot_general(
            row_eta[here, :], column_eta[...], (((1,), (1,)), ((), ())), preferred_element_type=F32
        )
        means = jnp.exp2(eta)
        high = means.astype(BF16)
        low = (means - high.astype(F32)).astype(BF16)
        w = weights[...]
        acc = jnp.dot(high, w, preferred_element_type=F32) + jnp.dot(low, w, preferred_element_type=F32)
        seen = jnp.dot(count_ref[here, :], w, preferred_element_type=F32)
        total = acc[:, :128] + acc[:, 128:]
        seen = seen[:, :128] + seen[:, 128:]
        return total - jnp.where(left_half(seen.shape), seen, 0.0)

    def updated(own, total):
        return own - STEP_CAP * jnp.tanh((total / (swap(total) + EPSILON)) / STEP_CAP)

    def factor_step(it):
        def chunk(j, carry):
            there = (x + far_first(j)) % X
            out = sums(u_eta, v_eta, v_sum, cnt, there * UCHUNK, UCHUNK)
            part_u[it, there] = out.reshape(YH, CO, UROWS, 128)
            send(it, U_CORE + j, part_u.at[it, there, :, 1 - co], core_in.at[it, j], gene_dev(0, 0, 1))
            return carry

        lax.fori_loop(0, X, chunk, 0)
        for j, dx in enumerate(FAR_FIRST):
            there = (x + dx) % X
            started.append((it, U_CORE + j, core_in.at[it, j]))
            arrived(it, U_CORE + j, core_in.at[it, j])
            sum_u[it, j] = part_u[it, there, :, co] + core_in[it, j]
            for dh in (1, 0):
                if dx or dh:
                    slot = dx * YH + dh
                    sent(it, U_CHIP + slot, sum_u.at[it, j, (yh + dh) % YH], chip_in.at[it, slot], gene_dev(dx, dh, 0))
        total = sum_u[it, len(FAR_FIRST) - 1, yh]
        for dx, dh in [(1, 0), (3, 0), (0, 1), (2, 0), (1, 1), (3, 1), (2, 1)]:
            slot = dx * YH + dh
            arrived(it, U_CHIP + slot, chip_in.at[it, slot])
            total = total + chip_in[it, slot]
        own_u[...] = updated(own_u[...], total)

    def loading_step(it):
        def chunk(j, carry):
            there = (zg + far_first(j)) % ZG
            out = sums(v_eta, u_eta, u_sum, cnt_t, there * VCHUNK, VCHUNK)
            part_v[it, there] = out.reshape(ZL, YL, VROWS, 128)
            send(it, V_PAIR + j, part_v.at[it, there, :, 1 - yl], pair_in.at[it, j], cell_dev(0, 0, 1))
            return carry

        lax.fori_loop(0, ZG, chunk, 0)
        for j, dg in enumerate(FAR_FIRST):
            there = (zg + dg) % ZG
            started.append((it, V_PAIR + j, pair_in.at[it, j]))
            arrived(it, V_PAIR + j, pair_in.at[it, j])
            sum1[it, j] = part_v[it, there, :, yl] + pair_in[it, j]
            for d in (3, 2, 1):
                sent(it, V_LINE + j * ZL + d, sum1.at[it, j, (zl + d) % ZL], line_in.at[it, j, d], cell_dev(0, d, 0))
        for j, dg in enumerate(FAR_FIRST):
            total = sum1[it, j, zl]
            for d in (1, 2, 3):
                arrived(it, V_LINE + j * ZL + d, line_in.at[it, j, d])
                total = total + line_in[it, j, d]
            if dg:
                sum2[it, j] = total
                sent(it, V_RING + dg, sum2.at[it, j], ring_in.at[it, dg], cell_dev(dg, 0, 0))
        for dg in (1, 3, 2):
            arrived(it, V_RING + dg, ring_in.at[it, dg])
            total = total + ring_in[it, dg]
        own_v[...] = updated(own_v[...], total)

    gather_v_start(0)
    gather_u_start(0)
    offset_columns(cell_ref[...] * LOG2E, RANK, RANK + 3, cell_cols)
    offset_columns(gene_ref[...] * LOG2E, RANK + 3, RANK, gene_cols)

    def prepare(k, carry):
        load(k).wait()
        rows = pl.ds(pl.multiple_of(k * 256, 256), 256)
        block = cnt32[rows, :].astype(F32)
        cnt[rows, :] = block.astype(BF16)
        cnt_t[:, rows] = block.T.astype(BF16)
        return carry

    gather_u_finish(0)
    lax.fori_loop(0, CELLS // 256, prepare, 0)
    gather_v_finish(0)
    assemble_u(0)
    assemble_v(0)
    for it in range(ITERS):
        factor_step(it)
        ubuf[it + 1, chip, co] = pack(own_u[...])
        if it + 1 == ITERS:
            new_rows[:UROWS] = own_u[...]
        gather_u_start(it + 1)
        gather_u_finish(it + 1)
        assemble_u(it + 1)
        loading_step(it)
        if it + 1 < ITERS:
            vbuf[it + 1, z, yl] = pack(own_v[...])
            gather_v_start(it + 1)
            gather_v_finish(it + 1)
            assemble_v(it + 1)
    new_rows[UROWS:] = own_v[...]
    for era, slot, src in started:
        pltpu.make_async_remote_copy(
            src_ref=src, dst_ref=src, send_sem=send_sem.at[era, slot],
            recv_sem=recv_sem.at[era, slot], device_id=(c, g), device_id_type=MESH,
        ).wait_send()


def per_device(counts, factors, loadings, cell_offset, gene_offset):
    vmem = pl.BlockSpec(memory_space=pltpu.VMEM)
    hbm = pl.BlockSpec(memory_space=pltpu.HBM)
    scratch = [
        pltpu.VMEM((UROWS, RANK), F32),
        pltpu.VMEM((VROWS, RANK), F32),
        pltpu.VMEM((1, CELLS), F32),
        pltpu.VMEM((1, GENES), F32),
        pltpu.VMEM((CELLS, GENES), jnp.int32),
        pltpu.VMEM((CELLS, GENES), BF16),
        pltpu.VMEM((GENES, CELLS), BF16),
        pltpu.VMEM((CELLS, 256), BF16),
        pltpu.VMEM((CELLS, 256), BF16),
        pltpu.VMEM((GENES, 256), BF16),
        pltpu.VMEM((GENES, 256), BF16),
        pltpu.VMEM((CELLS, 128), F32),
        pltpu.VMEM((GENES, 128), F32),
        pltpu.VMEM((UROWS, 128), F32),
        pltpu.VMEM((VROWS, 128), F32),
        pltpu.VMEM((ITERS + 1, X * YH, CO, UROWS // 2, 128), F32),
        pltpu.VMEM((ITERS, Z, YL, VROWS // 2, 128), F32),
        pltpu.VMEM((ITERS, X, YH, CO, UROWS, 128), F32),
        pltpu.VMEM((ITERS, X, YH, UROWS, 128), F32),
        pltpu.VMEM((ITERS, X, YH, UROWS, 128), F32),
        pltpu.VMEM((ITERS, X * YH, UROWS, 128), F32),
        pltpu.VMEM((ITERS, ZG, ZL, YL, VROWS, 128), F32),
        pltpu.VMEM((ITERS, ZG, ZL, VROWS, 128), F32),
        pltpu.VMEM((ITERS, ZG, ZL, VROWS, 128), F32),
        pltpu.VMEM((ITERS, ZG, ZL, VROWS, 128), F32),
        pltpu.VMEM((ITERS, ZG, VROWS, 128), F32),
        pltpu.VMEM((ITERS, ZG, VROWS, 128), F32),
        pltpu.SemaphoreType.DMA((CELLS // 256 + 4,)),
        pltpu.SemaphoreType.DMA((ITERS + 1, SLOTS)),
        pltpu.SemaphoreType.DMA((ITERS + 1, SLOTS)),
    ]
    rows = pl.pallas_call(
        kernel,
        name="sweeps",
        out_shape=jax.ShapeDtypeStruct((UROWS + VROWS, 128), F32),
        in_specs=[hbm] * 5,
        out_specs=vmem,
        scratch_shapes=scratch,
        compiler_params=pltpu.CompilerParams(
            collective_id=0, has_side_effects=True, vmem_limit_bytes=63 * 1024 * 1024
        ),
    )(counts, factors, loadings, cell_offset.reshape(1, -1), gene_offset.reshape(1, -1))
    return rows[:UROWS, :RANK], rows[UROWS:, :RANK]


def solution(mesh):
    in_specs = (
        P("cell", "gene"),
        P(("cell", "gene"), None),
        P(("gene", "cell"), None),
        P("cell"),
        P("gene"),
    )
    out_specs = (P(("cell", "gene"), None), P(("gene", "cell"), None))
    return jax.shard_map(
        per_device, mesh=mesh, in_specs=in_specs, out_specs=out_specs, check_vma=False
    )
```

```python
import functools

import jax
import jax.numpy as jnp
from jax import lax
from jax.experimental import pallas as pl
from jax.experimental.pallas import tpu as pltpu
from jax.sharding import PartitionSpec as P

ITERS = 2
EPSILON = 1e-06
STEP_CAP = 0.25
LOG2E = 1.4426950408889634
F32, BF16 = jnp.float32, jnp.bfloat16
MESH = pl.DeviceIdType.MESH

ZG, ZL, YL = 4, 4, 2
Z = ZG * ZL
X, YH, CO = 4, 2, 2
RANK = 64
UROWS, VROWS = 64, 32
CELLS = X * YH * CO * UROWS
GENES = ZG * ZL * YL * VROWS
UCHUNK = YH * CO * UROWS
VCHUNK = ZL * YL * VROWS
FAR_FIRST = (2, 1, 3, 0)
ZROWS = YL * VROWS
TILE = 256
NEAR = 2
U_CORE = 0
U_CHIP = U_CORE + X
V_PAIR = U_CHIP + X * YH
V_LINE = V_PAIR + ZG
V_RING = V_LINE + ZG * ZL
GU_CHIP = V_RING + ZG
GU_CORE = GU_CHIP + X * YH
GV_Z = GU_CORE + X * YH
GV_PAIR = GV_Z + ZG * ZL
SLOTS = GV_PAIR + ZG * ZL


def split(x):
    high = x.astype(BF16).astype(F32)
    return high, x - high


def left_half(shape):
    return lax.broadcasted_iota(jnp.int32, shape, len(shape) - 1) < RANK


def swap(x):
    return pltpu.roll(x, RANK, axis=x.ndim - 1)


def pairs(left, right):
    mask = left_half(left.shape)
    first = jnp.where(mask, left, swap(right))
    second = jnp.where(mask, swap(left), right)
    return first, second


def far_first(j):
    return (2 + 3 * j - (j * (j - 1)) // 2) % 4


def kernel(
    counts_hbm, u_hbm, v_hbm, cell_hbm, gene_hbm, new_rows,
    u_ref, v_ref, cell_ref, gene_ref, cnt32, cnt, cnt_t, u_eta, u_sum, v_eta, v_sum, cell_cols, gene_cols,
    own_u, own_v, ubuf, vbuf, part_u, core_in, sum_u, chip_in,
    part_v, pair_in, sum1, line_in, sum2, ring_in, load_sem, send_sem, recv_sem,
):
    c, g = lax.axis_index("cell"), lax.axis_index("gene")
    z, yl = c // YL, c % YL
    zg, zl = z // ZL, z % ZL
    chip, co = g // CO, g % CO
    x, yh = chip // YH, chip % YH

    def cell_dev(dg, dl, dy):
        there = ((zg + dg) % ZG) * ZL + (zl + dl) % ZL
        return (there * YL + (yl + dy) % YL, g)

    def gene_dev(dx, dh, dc):
        there = ((x + dx) % X) * YH + (yh + dh) % YH
        return (c, there * CO + (co + dc) % CO)

    def z_dev(d):
        return (((z + d) % Z) * YL + yl, g)

    far = [d for k in range(Z // 2, 0, -1) for d in dict.fromkeys((k, Z - k))]
    chips = [(dx, dh) for dx in FAR_FIRST for dh in (1, 0) if dx or dh]
    peers = [z_dev(d) for d in far] + [gene_dev(dx, dh, 0) for dx, dh in chips]
    peers += [cell_dev(0, 0, 1), gene_dev(0, 0, 1)]
    barrier = pltpu.get_barrier_semaphore()
    for peer in peers:
        pl.semaphore_signal(barrier, inc=1, device_id=peer, device_id_type=MESH)

    def load(k):
        rows = pl.ds(k * 256, 256)
        return pltpu.make_async_copy(counts_hbm.at[rows], cnt32.at[rows], load_sem.at[k])

    small = [
        pltpu.make_async_copy(src, dst, load_sem.at[CELLS // 256 + k])
        for k, (src, dst) in enumerate(
            ((v_hbm, v_ref), (u_hbm, u_ref), (cell_hbm, cell_ref), (gene_hbm, gene_ref))
        )
    ]
    for copy in small:
        copy.start()
    for k in range(CELLS // 256):
        load(k).start()

    started = []

    def send(era, slot, src, dst, device):
        copy = pltpu.make_async_remote_copy(
            src_ref=src, dst_ref=dst, send_sem=send_sem.at[era, slot],
            recv_sem=recv_sem.at[era, slot], device_id=device, device_id_type=MESH,
        )
        copy.start()

    def sent(era, slot, src, dst, device):
        send(era, slot, src, dst, device)
        started.append((era, slot, src))

    def arrived(era, slot, ref):
        pltpu.make_async_remote_copy(
            src_ref=ref, dst_ref=ref, send_sem=send_sem.at[era, slot],
            recv_sem=recv_sem.at[era, slot], device_id=(c, g), device_id_type=MESH,
        ).wait_recv()

    def pack(rows):
        half = rows.shape[0] // 2
        return jnp.where(left_half((half, 128)), rows[:half], swap(rows[half:]))

    own_u[...] = jnp.zeros_like(own_u)
    own_v[...] = jnp.zeros_like(own_v)
    for copy in small:
        copy.wait()
    own_u[:, :RANK] = u_ref[...]
    own_v[:, :RANK] = v_ref[...]

    def offset_columns(row, first_offset, first_one, turn, out):
        high, rest = split(row)
        mid, low = split(rest)
        index = lax.broadcasted_iota(jnp.int32, (128, row.shape[1]), 0)
        rows = jnp.zeros((128, row.shape[1]), F32)
        for k, part in enumerate((high, mid, low)):
            rows = jnp.where(index == first_offset + k, part, rows)
            rows = jnp.where(index == first_one + k, 1.0, rows)
        out[...] = (rows if turn is None else pltpu.roll(rows, turn, axis=1)).T

    ubuf[0, x, yh, co] = pack(own_u[...])
    vbuf[0, z, yl] = pack(own_v[...])
    pl.semaphore_wait(barrier, len(peers))

    def gather_u_start(era):
        mine = ubuf.at[era, x, yh, co]
        for dx, dh in chips:
            sent(era, GU_CHIP + dx * YH + dh, mine, mine, gene_dev(dx, dh, 0))
        sent(era, GU_CORE, mine, mine, gene_dev(0, 0, 1))

    def gather_u_forward(era):
        for dx, dh in [(1, 0), (3, 0), (0, 1), (2, 0), (1, 1), (3, 1), (2, 1)]:
            block = ubuf.at[era, (x - dx) % X, (yh - dh) % YH, co]
            arrived(era, GU_CHIP + dx * YH + dh, block)
            sent(era, GU_CORE + dx * YH + dh, block, block, gene_dev(0, 0, 1))

    def factor_tile(era, dx):
        for dh in range(YH):
            block = ubuf.at[era, (x - dx) % X, (yh - dh) % YH, 1 - co]
            arrived(era, GU_CORE + dx * YH + dh, block)
        there = (x - dx) % X
        packed = ubuf[era, there].reshape(YH * CO, UROWS // 2, 128)
        assemble(packed, there * TILE, u_eta, u_sum, cell_cols, True)
        return there

    def gather_v_start(era):
        mine = vbuf.at[era, z, yl]
        for d in far:
            sent(era, GV_Z + d, mine, mine, z_dev(d))
        sent(era, GV_PAIR, mine, mine, cell_dev(0, 0, 1))

    def gather_v_forward(era, first, last):
        for d in reversed(far):
            if first <= min(d, Z - d) <= last:
                block = vbuf.at[era, (z - d) % Z, yl]
                arrived(era, GV_Z + d, block)
                sent(era, GV_PAIR + d, block, block, cell_dev(0, 0, 1))

    def loading_tile(era, t):
        steps = range(4 * t - NEAR, 4 * t - NEAR + 4)
        for step in steps:
            arrived(era, GV_PAIR + (-step) % Z, vbuf.at[era, (z + step + Z) % Z, 1 - yl])
        packed = jnp.concatenate([vbuf[era, (z + step + Z) % Z] for step in steps], axis=0)
        assemble(packed, t * TILE, v_eta, v_sum, gene_cols, False)

    def assemble(packed, first_row, eta, total, columns, scale):
        rows = pl.ds(pl.multiple_of(first_row, TILE), TILE)
        plain_h, plain_l = split(packed)
        square_h, square_l = split(packed * packed)

        def put(ref, column, left, right):
            both = jnp.concatenate([half.astype(BF16) for half in pairs(left, right)], axis=1)
            ref[rows, column:column + 128] = both.reshape(TILE, 128)

        put(total, 0, plain_h, square_h)
        put(total, 128, plain_l, square_l)
        if scale:
            high, low = split(packed * LOG2E)
            put(eta, 0, high, low)
            third = high
        else:
            put(eta, 0, plain_h, plain_h)
            third = plain_l
        both = jnp.concatenate(pairs(third, third), axis=1).reshape(TILE, 128)
        eta[rows, 128:] = jnp.where(left_half(both.shape), both, columns[rows, :]).astype(BF16)

    def tile_sums(row_eta, column_eta, weights, count_ref, first, rows, tile):
        here = pl.ds(pl.multiple_of(first, rows), rows)
        there = pl.ds(pl.multiple_of(tile * TILE, TILE), TILE)
        eta = lax.dot_general(
            row_eta, column_eta[there, :], (((1,), (1,)), ((), ())), preferred_element_type=F32
        )
        means = jnp.exp2(eta)
        high = means.astype(BF16)
        low = (means - high.astype(F32)).astype(BF16)
        w = weights[there, :]
        acc = jnp.dot(high, w, preferred_element_type=F32) + jnp.dot(low, w, preferred_element_type=F32)
        return acc, jnp.dot(count_ref[here, there], w, preferred_element_type=F32)

    def add(first, second):
        return second if first is None else (first[0] + second[0], first[1] + second[1])

    def folded(sums):
        total, seen = (part[:, :128] + part[:, 128:] for part in sums)
        return total - jnp.where(left_half(seen.shape), seen, 0.0)

    def updated(own, total):
        return own - STEP_CAP * jnp.tanh((total / (swap(total) + EPSILON)) / STEP_CAP)

    def factor_part(it, j, sums):
        there = (x + far_first(j)) % X
        part_u[it, there] = folded(sums).reshape(YH, CO, UROWS, 128)
        send(it, U_CORE + j, part_u.at[it, there, :, 1 - co], core_in.at[it, j], gene_dev(0, 0, 1))

    def factor_tile_sums(j, tile):
        first = ((x + far_first(j)) % X) * UCHUNK
        rows = u_eta[pl.ds(pl.multiple_of(first, UCHUNK), UCHUNK), :]
        return tile_sums(rows, v_eta, v_sum, cnt, first, UCHUNK, tile)

    def factor_step(it):
        sums = None
        gather_v_forward(it, 1, 5)
        loading_tile(it, 0)
        sums = add(sums, factor_tile_sums(0, 0))
        gather_v_forward(it, 6, Z // 2)
        for t in (1, 3, 2):
            loading_tile(it, t)
            sums = add(sums, factor_tile_sums(0, t))
        factor_part(it, 0, sums)

        def chunk(j, carry):
            sums = None
            for t in range(GENES // TILE):
                sums = add(sums, factor_tile_sums(j, t))
            factor_part(it, j, sums)
            return carry

        lax.fori_loop(1, X, chunk, 0)
        for j, dx in enumerate(FAR_FIRST):
            there = (x + dx) % X
            started.append((it, U_CORE + j, core_in.at[it, j]))
            arrived(it, U_CORE + j, core_in.at[it, j])
            sum_u[it, j] = part_u[it, there, :, co] + core_in[it, j]
            for dh in (1, 0):
                if dx or dh:
                    slot = dx * YH + dh
                    sent(it, U_CHIP + slot, sum_u.at[it, j, (yh + dh) % YH], chip_in.at[it, slot], gene_dev(dx, dh, 0))
        total = sum_u[it, len(FAR_FIRST) - 1, yh]
        for dx, dh in [(1, 0), (3, 0), (0, 1), (2, 0), (1, 1), (3, 1), (2, 1)]:
            slot = dx * YH + dh
            arrived(it, U_CHIP + slot, chip_in.at[it, slot])
            total = total + chip_in[it, slot]
        own_u[...] = updated(own_u[...], total)

    def loading_part(it, j, sums):
        there = (zg + far_first(j)) % ZG
        part_v[it, there] = folded(sums).reshape(ZL, YL, VROWS, 128)
        send(it, V_PAIR + j, part_v.at[it, there, :, 1 - yl], pair_in.at[it, j], cell_dev(0, 0, 1))

    def loading_tile_sums(j, tile):
        there = (zg + far_first(j)) % ZG
        places = [((there * ZL + k + NEAR + Z - z) % Z) * ZROWS for k in range(ZL)]
        rows = jnp.concatenate([v_eta[pl.ds(pl.multiple_of(p, ZROWS), ZROWS), :] for p in places], axis=0)
        return tile_sums(rows, u_eta, u_sum, cnt_t, there * VCHUNK, VCHUNK, tile)

    def loading_step(it):
        sums = None
        gather_u_forward(it + 1)
        for dx in (0, 1, 3, 2):
            there = factor_tile(it + 1, dx)
            sums = add(sums, loading_tile_sums(0, there))
        loading_part(it, 0, sums)

        def chunk(j, carry):
            sums = None
            for t in range(CELLS // TILE):
                sums = add(sums, loading_tile_sums(j, t))
            loading_part(it, j, sums)
            return carry

        lax.fori_loop(1, ZG, chunk, 0)
        for j, dg in enumerate(FAR_FIRST):
            there = (zg + dg) % ZG
            started.append((it, V_PAIR + j, pair_in.at[it, j]))
            arrived(it, V_PAIR + j, pair_in.at[it, j])
            sum1[it, j] = part_v[it, there, :, yl] + pair_in[it, j]
            for d in (3, 2, 1):
                sent(it, V_LINE + j * ZL + d, sum1.at[it, j, (zl + d) % ZL], line_in.at[it, j, d], cell_dev(0, d, 0))
        for j, dg in enumerate(FAR_FIRST):
            total = sum1[it, j, zl]
            for d in (1, 2, 3):
                arrived(it, V_LINE + j * ZL + d, line_in.at[it, j, d])
                total = total + line_in[it, j, d]
            if dg:
                sum2[it, j] = total
                sent(it, V_RING + dg, sum2.at[it, j], ring_in.at[it, dg], cell_dev(dg, 0, 0))
        for dg in (1, 3, 2):
            arrived(it, V_RING + dg, ring_in.at[it, dg])
            total = total + ring_in[it, dg]
        own_v[...] = updated(own_v[...], total)

    turn = ((NEAR + Z - z) * ZROWS) % GENES
    gather_v_start(0)
    gather_u_start(0)
    offset_columns(cell_ref[...] * LOG2E, RANK, RANK + 3, None, cell_cols)
    offset_columns(gene_ref[...] * LOG2E, RANK + 3, RANK, turn, gene_cols)

    def prepare(k, carry):
        load(k).wait()
        rows = pl.ds(pl.multiple_of(k * 256, 256), 256)
        block = cnt32[rows, :].astype(F32)
        cnt[rows, :] = pltpu.roll(block, turn, axis=1).astype(BF16)
        cnt_t[:, rows] = block.T.astype(BF16)
        return carry

    lax.fori_loop(0, CELLS // 256, prepare, 0)
    gather_u_forward(0)
    for dx in (0, 1, 3, 2):
        factor_tile(0, dx)
    for it in range(ITERS):
        factor_step(it)
        ubuf[it + 1, x, yh, co] = pack(own_u[...])
        if it + 1 == ITERS:
            new_rows[:UROWS] = own_u[...]
        gather_u_start(it + 1)
        loading_step(it)
        if it + 1 < ITERS:
            vbuf[it + 1, z, yl] = pack(own_v[...])
            gather_v_start(it + 1)
    new_rows[UROWS:] = own_v[...]
    for era, slot, src in started:
        pltpu.make_async_remote_copy(
            src_ref=src, dst_ref=src, send_sem=send_sem.at[era, slot],
            recv_sem=recv_sem.at[era, slot], device_id=(c, g), device_id_type=MESH,
        ).wait_send()


def per_device(counts, factors, loadings, cell_offset, gene_offset):
    arrays = (counts, factors, loadings, cell_offset.reshape(1, -1), gene_offset.reshape(1, -1))
    vmem = pl.BlockSpec(memory_space=pltpu.VMEM)
    hbm = pl.BlockSpec(memory_space=pltpu.HBM)
    scratch = [
        pltpu.VMEM((UROWS, RANK), F32),
        pltpu.VMEM((VROWS, RANK), F32),
        pltpu.VMEM((1, CELLS), F32),
        pltpu.VMEM((1, GENES), F32),
        pltpu.VMEM((CELLS, GENES), jnp.int32),
        pltpu.VMEM((CELLS, GENES), BF16),
        pltpu.VMEM((GENES, CELLS), BF16),
        pltpu.VMEM((CELLS, 256), BF16),
        pltpu.VMEM((CELLS, 256), BF16),
        pltpu.VMEM((GENES, 256), BF16),
        pltpu.VMEM((GENES, 256), BF16),
        pltpu.VMEM((CELLS, 128), F32),
        pltpu.VMEM((GENES, 128), F32),
        pltpu.VMEM((UROWS, 128), F32),
        pltpu.VMEM((VROWS, 128), F32),
        pltpu.VMEM((ITERS + 1, X, YH, CO, UROWS // 2, 128), F32),
        pltpu.VMEM((ITERS, Z, YL, VROWS // 2, 128), F32),
        pltpu.VMEM((ITERS, X, YH, CO, UROWS, 128), F32),
        pltpu.VMEM((ITERS, X, YH, UROWS, 128), F32),
        pltpu.VMEM((ITERS, X, YH, UROWS, 128), F32),
        pltpu.VMEM((ITERS, X * YH, UROWS, 128), F32),
        pltpu.VMEM((ITERS, ZG, ZL, YL, VROWS, 128), F32),
        pltpu.VMEM((ITERS, ZG, ZL, VROWS, 128), F32),
        pltpu.VMEM((ITERS, ZG, ZL, VROWS, 128), F32),
        pltpu.VMEM((ITERS, ZG, ZL, VROWS, 128), F32),
        pltpu.VMEM((ITERS, ZG, VROWS, 128), F32),
        pltpu.VMEM((ITERS, ZG, VROWS, 128), F32),
        pltpu.SemaphoreType.DMA((CELLS // 256 + 4,)),
        pltpu.SemaphoreType.DMA((ITERS + 1, SLOTS)),
        pltpu.SemaphoreType.DMA((ITERS + 1, SLOTS)),
    ]
    rows = pl.pallas_call(
        kernel,
        name="sweeps",
        out_shape=jax.ShapeDtypeStruct((UROWS + VROWS, 128), F32),
        in_specs=[hbm] * 5,
        out_specs=vmem,
        scratch_shapes=scratch,
        compiler_params=pltpu.CompilerParams(
            collective_id=0, has_side_effects=True, vmem_limit_bytes=48 * 1024 * 1024
        ),
    )(*(pltpu.with_memory_space_constraint(a, pltpu.HBM) for a in arrays))
    return rows[:UROWS, :RANK], rows[UROWS:, :RANK]


def solution(mesh):
    in_specs = (
        P("cell", "gene"),
        P(("cell", "gene"), None),
        P(("gene", "cell"), None),
        P("cell"),
        P("gene"),
    )
    out_specs = (P(("cell", "gene"), None), P(("gene", "cell"), None))
    return jax.shard_map(
        per_device, mesh=mesh, in_specs=in_specs, out_specs=out_specs, check_vma=False
    )
```

```python
import functools

import jax
import jax.numpy as jnp
from jax import lax
from jax.experimental import pallas as pl
from jax.experimental.pallas import tpu as pltpu
from jax.sharding import PartitionSpec as P

ITERS = 2
EPSILON = 1e-06
STEP_CAP = 0.25
LOG2E = 1.4426950408889634
F32, BF16 = jnp.float32, jnp.bfloat16
MESH = pl.DeviceIdType.MESH

ZG, ZL, YL = 4, 4, 2
Z = ZG * ZL
X, YH, CO = 4, 2, 2
RANK = 64
UROWS, VROWS = 64, 32
CELLS = X * YH * CO * UROWS
GENES = ZG * ZL * YL * VROWS
UCHUNK = YH * CO * UROWS
VCHUNK = ZL * YL * VROWS
FAR_FIRST = (2, 1, 3, 0)
ZROWS = YL * VROWS
TILE = 256
NEAR = 2
U_CORE = 0
U_CHIP = U_CORE + X
V_PAIR = U_CHIP + X * YH
V_LINE = V_PAIR + ZG * ZL
V_RING = V_LINE + ZG * ZL
GU_CHIP = V_RING + ZG
GU_CORE = GU_CHIP + X * YH
GV_Z = GU_CORE + X * YH
GV_PAIR = GV_Z + ZG * ZL
SLOTS = GV_PAIR + ZG * ZL


def split(x):
    high = x.astype(BF16).astype(F32)
    return high, x - high


def left_half(shape):
    return lax.broadcasted_iota(jnp.int32, shape, len(shape) - 1) < RANK


def swap(x):
    return pltpu.roll(x, RANK, axis=x.ndim - 1)


def pairs(left, right):
    mask = left_half(left.shape)
    first = jnp.where(mask, left, swap(right))
    second = jnp.where(mask, swap(left), right)
    return first, second


def kernel(
    counts_hbm, u_hbm, v_hbm, cell_hbm, gene_hbm, new_rows,
    u_ref, v_ref, cell_ref, gene_ref, cnt32, cnt, cnt_t, u_eta, u_sum, v_eta, v_sum, cell_cols, gene_cols,
    own_u, own_v, ubuf, vbuf, part_u, core_in, sum_u, chip_in,
    part_v, pair_in, sum1, line_in, sum2, ring_in, load_sem, send_sem, recv_sem,
):
    c, g = lax.axis_index("cell"), lax.axis_index("gene")
    z, yl = c // YL, c % YL
    zg, zl = z // ZL, z % ZL
    chip, co = g // CO, g % CO
    x, yh = chip // YH, chip % YH

    def cell_dev(dg, dl, dy):
        there = ((zg + dg) % ZG) * ZL + (zl + dl) % ZL
        return (there * YL + (yl + dy) % YL, g)

    def gene_dev(dx, dh, dc):
        there = ((x + dx) % X) * YH + (yh + dh) % YH
        return (c, there * CO + (co + dc) % CO)

    def z_dev(d):
        return (((z + d) % Z) * YL + yl, g)

    far = [d for k in range(Z // 2, 0, -1) for d in dict.fromkeys((k, Z - k))]
    chips = [(dx, dh) for dx in FAR_FIRST for dh in (1, 0) if dx or dh]
    peers = [z_dev(d) for d in far] + [gene_dev(dx, dh, 0) for dx, dh in chips]
    peers += [cell_dev(0, 0, 1), gene_dev(0, 0, 1)]
    barrier = pltpu.get_barrier_semaphore()
    for peer in peers:
        pl.semaphore_signal(barrier, inc=1, device_id=peer, device_id_type=MESH)

    def load(k):
        rows = pl.ds(k * 256, 256)
        return pltpu.make_async_copy(counts_hbm.at[rows], cnt32.at[rows], load_sem.at[k])

    small = [
        pltpu.make_async_copy(src, dst, load_sem.at[CELLS // 256 + k])
        for k, (src, dst) in enumerate(
            ((v_hbm, v_ref), (u_hbm, u_ref), (cell_hbm, cell_ref), (gene_hbm, gene_ref))
        )
    ]
    for copy in small:
        copy.start()
    for k in range(CELLS // 256):
        load(k).start()

    started = []

    def sent(era, slot, src, dst, device):
        copy = pltpu.make_async_remote_copy(
            src_ref=src, dst_ref=dst, send_sem=send_sem.at[era, slot],
            recv_sem=recv_sem.at[era, slot], device_id=device, device_id_type=MESH,
        )
        copy.start()
        started.append((era, slot, src))

    def arrived(era, slot, ref):
        pltpu.make_async_remote_copy(
            src_ref=ref, dst_ref=ref, send_sem=send_sem.at[era, slot],
            recv_sem=recv_sem.at[era, slot], device_id=(c, g), device_id_type=MESH,
        ).wait_recv()

    def pack(rows):
        half = rows.shape[0] // 2
        return jnp.where(left_half((half, 128)), rows[:half], swap(rows[half:]))

    own_u[...] = jnp.zeros_like(own_u)
    own_v[...] = jnp.zeros_like(own_v)
    for copy in small:
        copy.wait()
    own_u[:, :RANK] = u_ref[...]
    own_v[:, :RANK] = v_ref[...]

    def offset_columns(row, first_offset, first_one, turn, out):
        high, rest = split(row)
        mid, low = split(rest)
        index = lax.broadcasted_iota(jnp.int32, (128, row.shape[1]), 0)
        rows = jnp.zeros((128, row.shape[1]), F32)
        for k, part in enumerate((high, mid, low)):
            rows = jnp.where(index == first_offset + k, part, rows)
            rows = jnp.where(index == first_one + k, 1.0, rows)
        out[...] = (rows if turn is None else pltpu.roll(rows, turn, axis=1)).T

    ubuf[0, x, yh, co] = pack(own_u[...])
    vbuf[0, z, yl] = pack(own_v[...])
    pl.semaphore_wait(barrier, len(peers))

    def gather_u_start(era):
        mine = ubuf.at[era, x, yh, co]
        for dx, dh in chips:
            sent(era, GU_CHIP + dx * YH + dh, mine, mine, gene_dev(dx, dh, 0))
        sent(era, GU_CORE, mine, mine, gene_dev(0, 0, 1))

    def gather_u_forward(era):
        for dx, dh in [(1, 0), (3, 0), (0, 1), (2, 0), (1, 1), (3, 1), (2, 1)]:
            block = ubuf.at[era, (x - dx) % X, (yh - dh) % YH, co]
            arrived(era, GU_CHIP + dx * YH + dh, block)
            sent(era, GU_CORE + dx * YH + dh, block, block, gene_dev(0, 0, 1))

    def factor_tile(era, dx):
        for dh in range(YH):
            block = ubuf.at[era, (x - dx) % X, (yh - dh) % YH, 1 - co]
            arrived(era, GU_CORE + dx * YH + dh, block)
        there = (x - dx) % X
        packed = ubuf[era, there].reshape(YH * CO, UROWS // 2, 128)
        assemble(packed, there * TILE, u_eta, u_sum, cell_cols, True)
        return there

    def gather_v_start(era):
        mine = vbuf.at[era, z, yl]
        for d in far:
            sent(era, GV_Z + d, mine, mine, z_dev(d))
        sent(era, GV_PAIR, mine, mine, cell_dev(0, 0, 1))

    def gather_v_forward(era, first, last):
        for d in reversed(far):
            if first <= min(d, Z - d) <= last:
                block = vbuf.at[era, (z - d) % Z, yl]
                arrived(era, GV_Z + d, block)
                sent(era, GV_PAIR + d, block, block, cell_dev(0, 0, 1))

    def loading_tile(era, t):
        steps = range(4 * t - NEAR, 4 * t - NEAR + 4)
        for step in steps:
            arrived(era, GV_PAIR + (-step) % Z, vbuf.at[era, (z + step + Z) % Z, 1 - yl])
        packed = jnp.concatenate([vbuf[era, (z + step + Z) % Z] for step in steps], axis=0)
        assemble(packed, t * TILE, v_eta, v_sum, gene_cols, False)

    def assemble(packed, first_row, eta, total, columns, scale):
        rows = pl.ds(pl.multiple_of(first_row, TILE), TILE)
        plain_h, plain_l = split(packed)
        square_h, square_l = split(packed * packed)

        def put(ref, column, left, right):
            both = jnp.concatenate([half.astype(BF16) for half in pairs(left, right)], axis=1)
            ref[rows, column:column + 128] = both.reshape(TILE, 128)

        put(total, 0, plain_h, square_h)
        put(total, 128, plain_l, square_l)
        if scale:
            high, low = split(packed * LOG2E)
            put(eta, 0, high, low)
            third = high
        else:
            put(eta, 0, plain_h, plain_h)
            third = plain_l
        both = jnp.concatenate(pairs(third, third), axis=1).reshape(TILE, 128)
        eta[rows, 128:] = jnp.where(left_half(both.shape), both, columns[rows, :]).astype(BF16)

    def products(row_eta, column_eta, weights, count_ref, first, rows, columns):
        here = pl.ds(pl.multiple_of(first, rows), rows)
        eta = lax.dot_general(
            row_eta, column_eta[columns, :], (((1,), (1,)), ((), ())), preferred_element_type=F32
        )
        means = jnp.exp2(eta)
        high = means.astype(BF16)
        low = (means - high.astype(F32)).astype(BF16)
        stacked = jnp.concatenate([high, low, count_ref[here, columns]], axis=0)
        return jnp.dot(stacked, weights[columns, :], preferred_element_type=F32)

    def folded(sums):
        high, low, seen = (part[:, :128] + part[:, 128:] for part in jnp.split(sums, 3, axis=0))
        return high + low - jnp.where(left_half(seen.shape), seen, 0.0)

    def updated(own, total):
        return own - STEP_CAP * jnp.tanh((total / (swap(total) + EPSILON)) / STEP_CAP)

    def factor_part(it, j, sums):
        there = (x + FAR_FIRST[j]) % X
        part_u[it, there] = folded(sums).reshape(YH, CO, UROWS, 128)
        sent(it, U_CORE + j, part_u.at[it, there, :, 1 - co], core_in.at[it, j], gene_dev(0, 0, 1))

    def factor_products(j, columns):
        first = ((x + FAR_FIRST[j]) % X) * UCHUNK
        rows = u_eta[pl.ds(pl.multiple_of(first, UCHUNK), UCHUNK), :]
        return products(rows, v_eta, v_sum, cnt, first, UCHUNK, columns)

    def factor_step(it):
        gather_v_forward(it, 1, Z // 2)
        sums = None
        for t in (0, 1, 3, 2):
            loading_tile(it, t)
            part = factor_products(0, pl.ds(t * TILE, TILE))
            sums = part if sums is None else sums + part
        factor_part(it, 0, sums)
        for j in range(1, X):
            factor_part(it, j, factor_products(j, pl.ds(0, GENES)))
        for j, dx in enumerate(FAR_FIRST):
            there = (x + dx) % X
            arrived(it, U_CORE + j, core_in.at[it, j])
            sum_u[it, j] = part_u[it, there, :, co] + core_in[it, j]
            for dh in (1, 0):
                if dx or dh:
                    slot = dx * YH + dh
                    sent(it, U_CHIP + slot, sum_u.at[it, j, (yh + dh) % YH], chip_in.at[it, slot], gene_dev(dx, dh, 0))
        total = sum_u[it, len(FAR_FIRST) - 1, yh]
        for dx, dh in [(1, 0), (3, 0), (0, 1), (2, 0), (1, 1), (3, 1), (2, 1)]:
            slot = dx * YH + dh
            arrived(it, U_CHIP + slot, chip_in.at[it, slot])
            total = total + chip_in[it, slot]
        own_u[...] = updated(own_u[...], total)

    def loading_part(it, j, sums):
        there = (zg + FAR_FIRST[j]) % ZG
        part_v[it, there] = folded(sums).reshape(ZL, YL, VROWS, 128)
        for d in (2, 3, 1, 0):
            piece = part_v.at[it, there, (zl + d) % ZL, 1 - yl]
            sent(it, V_PAIR + j * ZL + d, piece, pair_in.at[it, j, d], cell_dev(0, 0, 1))

    def loading_products(j):
        there = (zg + FAR_FIRST[j]) % ZG
        places = [((there * ZL + k + NEAR + Z - z) % Z) * ZROWS for k in range(ZL)]
        rows = jnp.concatenate([v_eta[pl.ds(pl.multiple_of(p, ZROWS), ZROWS), :] for p in places], axis=0)
        return products(rows, u_eta, u_sum, cnt_t, there * VCHUNK, VCHUNK, pl.ds(0, CELLS))

    def loading_step(it):
        gather_u_forward(it + 1)
        for dx in (0, 1, 3, 2):
            factor_tile(it + 1, dx)
        for j in range(ZG):
            loading_part(it, j, loading_products(j))
        for j, dg in enumerate(FAR_FIRST):
            there = (zg + dg) % ZG
            for d in (2, 3, 1, 0):
                arrived(it, V_PAIR + j * ZL + d, pair_in.at[it, j, d])
                sum1[it, j, d] = part_v[it, there, (zl + d) % ZL, yl] + pair_in[it, j, d]
                if d:
                    sent(it, V_LINE + j * ZL + d, sum1.at[it, j, d], line_in.at[it, j, d], cell_dev(0, d, 0))
        for j, dg in enumerate(FAR_FIRST):
            total = sum1[it, j, 0]
            for d in (1, 2, 3):
                arrived(it, V_LINE + j * ZL + d, line_in.at[it, j, d])
                total = total + line_in[it, j, d]
            if dg:
                sum2[it, j] = total
                sent(it, V_RING + dg, sum2.at[it, j], ring_in.at[it, dg], cell_dev(dg, 0, 0))
        for dg in (1, 3, 2):
            arrived(it, V_RING + dg, ring_in.at[it, dg])
            total = total + ring_in[it, dg]
        own_v[...] = updated(own_v[...], total)

    turn = ((NEAR + Z - z) * ZROWS) % GENES
    gather_v_start(0)
    gather_u_start(0)
    offset_columns(cell_ref[...] * LOG2E, RANK, RANK + 3, None, cell_cols)
    offset_columns(gene_ref[...] * LOG2E, RANK + 3, RANK, turn, gene_cols)

    def prepare(k, carry):
        load(k).wait()
        rows = pl.ds(pl.multiple_of(k * 256, 256), 256)
        block = cnt32[rows, :].astype(F32)
        cnt[rows, :] = pltpu.roll(block, turn, axis=1).astype(BF16)
        cnt_t[:, rows] = block.T.astype(BF16)
        return carry

    lax.fori_loop(0, CELLS // 256, prepare, 0)
    gather_u_forward(0)
    for dx in (0, 1, 3, 2):
        factor_tile(0, dx)
    for it in range(ITERS):
        factor_step(it)
        ubuf[it + 1, x, yh, co] = pack(own_u[...])
        if it + 1 == ITERS:
            new_rows[:UROWS] = own_u[...]
        gather_u_start(it + 1)
        loading_step(it)
        if it + 1 < ITERS:
            vbuf[it + 1, z, yl] = pack(own_v[...])
            gather_v_start(it + 1)
    new_rows[UROWS:] = own_v[...]
    for era, slot, src in started:
        pltpu.make_async_remote_copy(
            src_ref=src, dst_ref=src, send_sem=send_sem.at[era, slot],
            recv_sem=recv_sem.at[era, slot], device_id=(c, g), device_id_type=MESH,
        ).wait_send()


def per_device(counts, factors, loadings, cell_offset, gene_offset):
    arrays = (counts, factors, loadings, cell_offset.reshape(1, -1), gene_offset.reshape(1, -1))
    vmem = pl.BlockSpec(memory_space=pltpu.VMEM)
    hbm = pl.BlockSpec(memory_space=pltpu.HBM)
    scratch = [
        pltpu.VMEM((UROWS, RANK), F32),
        pltpu.VMEM((VROWS, RANK), F32),
        pltpu.VMEM((1, CELLS), F32),
        pltpu.VMEM((1, GENES), F32),
        pltpu.VMEM((CELLS, GENES), jnp.int32),
        pltpu.VMEM((CELLS, GENES), BF16),
        pltpu.VMEM((GENES, CELLS), BF16),
        pltpu.VMEM((CELLS, 256), BF16),
        pltpu.VMEM((CELLS, 256), BF16),
        pltpu.VMEM((GENES, 256), BF16),
        pltpu.VMEM((GENES, 256), BF16),
        pltpu.VMEM((CELLS, 128), F32),
        pltpu.VMEM((GENES, 128), F32),
        pltpu.VMEM((UROWS, 128), F32),
        pltpu.VMEM((VROWS, 128), F32),
        pltpu.VMEM((ITERS + 1, X, YH, CO, UROWS // 2, 128), F32),
        pltpu.VMEM((ITERS, Z, YL, VROWS // 2, 128), F32),
        pltpu.VMEM((ITERS, X, YH, CO, UROWS, 128), F32),
        pltpu.VMEM((ITERS, X, YH, UROWS, 128), F32),
        pltpu.VMEM((ITERS, X, YH, UROWS, 128), F32),
        pltpu.VMEM((ITERS, X * YH, UROWS, 128), F32),
        pltpu.VMEM((ITERS, ZG, ZL, YL, VROWS, 128), F32),
        pltpu.VMEM((ITERS, ZG, ZL, VROWS, 128), F32),
        pltpu.VMEM((ITERS, ZG, ZL, VROWS, 128), F32),
        pltpu.VMEM((ITERS, ZG, ZL, VROWS, 128), F32),
        pltpu.VMEM((ITERS, ZG, VROWS, 128), F32),
        pltpu.VMEM((ITERS, ZG, VROWS, 128), F32),
        pltpu.SemaphoreType.DMA((CELLS // 256 + 4,)),
        pltpu.SemaphoreType.DMA((ITERS + 1, SLOTS)),
        pltpu.SemaphoreType.DMA((ITERS + 1, SLOTS)),
    ]
    rows = pl.pallas_call(
        kernel,
        name="sweeps",
        out_shape=jax.ShapeDtypeStruct((UROWS + VROWS, 128), F32),
        in_specs=[hbm] * 5,
        out_specs=vmem,
        scratch_shapes=scratch,
        compiler_params=pltpu.CompilerParams(
            collective_id=0, has_side_effects=True, vmem_limit_bytes=48 * 1024 * 1024
        ),
    )(*(pltpu.with_memory_space_constraint(a, pltpu.HBM) for a in arrays))
    return rows[:UROWS, :RANK], rows[UROWS:, :RANK]


def solution(mesh):
    in_specs = (
        P("cell", "gene"),
        P(("cell", "gene"), None),
        P(("gene", "cell"), None),
        P("cell"),
        P("gene"),
    )
    out_specs = (P(("cell", "gene"), None), P(("gene", "cell"), None))
    return jax.shard_map(
        per_device, mesh=mesh, in_specs=in_specs, out_specs=out_specs, check_vma=False
    )
```

```python
import functools

import jax
import jax.numpy as jnp
from jax import lax
from jax.experimental import pallas as pl
from jax.experimental.pallas import tpu as pltpu
from jax.sharding import PartitionSpec as P

ITERS = 2
EPSILON = 1e-06
STEP_CAP = 0.25
LOG2E = 1.4426950408889634
F32, BF16 = jnp.float32, jnp.bfloat16
MESH = pl.DeviceIdType.MESH

ZG, ZL, YL = 4, 4, 2
Z = ZG * ZL
X, YH, CO = 4, 2, 2
RANK = 64
UROWS, VROWS = 64, 32
CELLS = X * YH * CO * UROWS
GENES = ZG * ZL * YL * VROWS
UCHUNK = YH * CO * UROWS
VCHUNK = ZL * YL * VROWS
FAR_FIRST = (2, 1, 3, 0)
TILE = 256
U_CORE = 0
U_CHIP = U_CORE + X
V_PAIR = U_CHIP + X * YH
V_LINE = V_PAIR + ZG * ZL
V_RING = V_LINE + ZG * ZL
GU_CHIP = V_RING + ZG
GU_CORE = GU_CHIP + X * YH
GV_Z = GU_CORE + X * YH
GV_PAIR = GV_Z + ZG * ZL
SLOTS = GV_PAIR + ZG * ZL


def split(x):
    high = x.astype(BF16).astype(F32)
    return high, x - high


def left_half(shape):
    return lax.broadcasted_iota(jnp.int32, shape, len(shape) - 1) < RANK


def swap(x):
    return pltpu.roll(x, RANK, axis=x.ndim - 1)


def pairs(left, right):
    mask = left_half(left.shape)
    first = jnp.where(mask, left, swap(right))
    second = jnp.where(mask, swap(left), right)
    return first, second


def near_first(t):
    return t + t // 2 - 2 * (t // 3)


def far_first(j):
    return (2 + 3 * j - (j * (j - 1)) // 2) % 4


def kernel(
    counts_hbm, u_hbm, v_hbm, cell_hbm, gene_hbm, new_rows,
    u_ref, v_ref, cell_ref, gene_ref, cnt32, cnt, cnt_t, u_eta, u_sum, v_eta, v_sum, cell_cols, gene_cols,
    own_u, own_v, ubuf, vbuf, part_u, core_in, sum_u, chip_in,
    part_v, pair_in, sum1, line_in, sum2, ring_in, load_sem, send_sem, recv_sem,
):
    c, g = lax.axis_index("cell"), lax.axis_index("gene")
    z, yl = c // YL, c % YL
    zg, zl = z // ZL, z % ZL
    chip, co = g // CO, g % CO
    x, yh = chip // YH, chip % YH

    def cell_dev(dg, dl, dy):
        there = ((zg + dg) % ZG) * ZL + (zl + dl) % ZL
        return (there * YL + (yl + dy) % YL, g)

    def gene_dev(dx, dh, dc):
        there = ((x + dx) % X) * YH + (yh + dh) % YH
        return (c, there * CO + (co + dc) % CO)

    def z_dev(d):
        return (((z + d) % Z) * YL + yl, g)

    far = [d for k in range(Z // 2, 0, -1) for d in dict.fromkeys((k, Z - k))]
    chips = [(dx, dh) for dx in FAR_FIRST for dh in (1, 0) if dx or dh]
    peers = [z_dev(d) for d in far] + [gene_dev(dx, dh, 0) for dx, dh in chips]
    peers += [cell_dev(0, 0, 1), gene_dev(0, 0, 1)]
    barrier = pltpu.get_barrier_semaphore()
    for peer in peers:
        pl.semaphore_signal(barrier, inc=1, device_id=peer, device_id_type=MESH)

    def load(k):
        rows = pl.ds(k * 256, 256)
        return pltpu.make_async_copy(counts_hbm.at[rows], cnt32.at[rows], load_sem.at[k])

    small = [
        pltpu.make_async_copy(src, dst, load_sem.at[CELLS // 256 + k])
        for k, (src, dst) in enumerate(
            ((v_hbm, v_ref), (u_hbm, u_ref), (cell_hbm, cell_ref), (gene_hbm, gene_ref))
        )
    ]
    for copy in small:
        copy.start()
    for k in range(CELLS // 256):
        load(k).start()

    started = []

    def send(era, slot, src, dst, device):
        copy = pltpu.make_async_remote_copy(
            src_ref=src, dst_ref=dst, send_sem=send_sem.at[era, slot],
            recv_sem=recv_sem.at[era, slot], device_id=device, device_id_type=MESH,
        )
        copy.start()

    def sent(era, slot, src, dst, device):
        send(era, slot, src, dst, device)
        started.append((era, slot, src))

    def take():
        pending = list(started)
        started.clear()
        return pending

    def drain(pending):
        for era, slot, src in pending:
            pltpu.make_async_remote_copy(
                src_ref=src, dst_ref=src, send_sem=send_sem.at[era, slot],
                recv_sem=recv_sem.at[era, slot], device_id=(c, g), device_id_type=MESH,
            ).wait_send()

    def arrived(era, slot, ref):
        pltpu.make_async_remote_copy(
            src_ref=ref, dst_ref=ref, send_sem=send_sem.at[era, slot],
            recv_sem=recv_sem.at[era, slot], device_id=(c, g), device_id_type=MESH,
        ).wait_recv()

    def pack(rows):
        half = rows.shape[0] // 2
        return jnp.where(left_half((half, 128)), rows[:half], swap(rows[half:]))

    own_u[...] = jnp.zeros_like(own_u)
    own_v[...] = jnp.zeros_like(own_v)
    for copy in small:
        copy.wait()
    own_u[:, :RANK] = u_ref[...]
    own_v[:, :RANK] = v_ref[...]

    def offset_columns(row, first_offset, first_one, out):
        high, rest = split(row)
        mid, low = split(rest)
        index = lax.broadcasted_iota(jnp.int32, (128, row.shape[1]), 0)
        rows = jnp.zeros((128, row.shape[1]), F32)
        for k, part in enumerate((high, mid, low)):
            rows = jnp.where(index == first_offset + k, part, rows)
            rows = jnp.where(index == first_one + k, 1.0, rows)
        out[...] = rows.T

    ubuf[0, x, yh, co] = pack(own_u[...])
    vbuf[0, z, yl] = pack(own_v[...])
    pl.semaphore_wait(barrier, len(peers))

    def gather_u_start(era):
        mine = ubuf.at[era, x, yh, co]
        for dx, dh in chips:
            sent(era, GU_CHIP + dx * YH + dh, mine, mine, gene_dev(dx, dh, 0))
        sent(era, GU_CORE, mine, mine, gene_dev(0, 0, 1))

    def gather_u_forward(era):
        for dx, dh in [(1, 0), (3, 0), (0, 1), (2, 0), (1, 1), (3, 1), (2, 1)]:
            block = ubuf.at[era, (x - dx) % X, (yh - dh) % YH, co]
            arrived(era, GU_CHIP + dx * YH + dh, block)
            sent(era, GU_CORE + dx * YH + dh, block, block, gene_dev(0, 0, 1))

    def gather_u_finish(era):
        def tile(t, carry):
            dx = near_first(t)
            there = (x - dx + X) % X
            for dh in range(YH):
                arrived(era, GU_CORE + dx * YH + dh, ubuf.at[era, there, (yh - dh) % YH, 1 - co])
            packed = ubuf[era, there].reshape(YH * CO, UROWS // 2, 128)
            assemble(packed, there * TILE, u_eta, u_sum, cell_cols, True)
            return carry

        lax.fori_loop(0, X, tile, 0)

    def gather_v_start(era):
        mine = vbuf.at[era, z, yl]
        for d in far:
            sent(era, GV_Z + d, mine, mine, z_dev(d))
        sent(era, GV_PAIR, mine, mine, cell_dev(0, 0, 1))

    def gather_v_forward(era):
        for d in reversed(far):
            block = vbuf.at[era, (z - d) % Z, yl]
            arrived(era, GV_Z + d, block)
            sent(era, GV_PAIR + d, block, block, cell_dev(0, 0, 1))

    def gather_v_finish(era):
        def tile(t, carry):
            there = (zg + near_first(t)) % ZG
            for k in range(ZL):
                source = there * ZL + k
                arrived(era, GV_PAIR + (z - source + Z) % Z, vbuf.at[era, source, 1 - yl])
            packed = vbuf[era, pl.ds(there * ZL, ZL)].reshape(ZL * YL, VROWS // 2, 128)
            assemble(packed, there * TILE, v_eta, v_sum, gene_cols, False)
            return carry

        lax.fori_loop(0, ZG, tile, 0)

    def assemble(packed, first_row, eta, total, columns, scale):
        rows = pl.ds(pl.multiple_of(first_row, TILE), TILE)
        plain_h, plain_l = split(packed)
        square_h, square_l = split(packed * packed)

        def put(ref, column, left, right):
            both = jnp.concatenate([half.astype(BF16) for half in pairs(left, right)], axis=1)
            ref[rows, column:column + 128] = both.reshape(TILE, 128)

        put(total, 0, plain_h, square_h)
        put(total, 128, plain_l, square_l)
        if scale:
            high, low = split(packed * LOG2E)
            put(eta, 0, high, low)
            third = high
        else:
            put(eta, 0, plain_h, plain_h)
            third = plain_l
        both = jnp.concatenate(pairs(third, third), axis=1).reshape(TILE, 128)
        eta[rows, 128:] = jnp.where(left_half(both.shape), both, columns[rows, :]).astype(BF16)

    def sums(row_eta, column_eta, weights, count_ref, first, rows):
        here = pl.ds(pl.multiple_of(first, rows), rows)
        eta = lax.dot_general(
            row_eta[here, :], column_eta[...], (((1,), (1,)), ((), ())), preferred_element_type=F32
        )
        means = jnp.exp2(eta)
        high = means.astype(BF16)
        low = (means - high.astype(F32)).astype(BF16)
        stacked = jnp.concatenate([high, low, count_ref[here, :]], axis=0)
        out = jnp.dot(stacked, weights[...], preferred_element_type=F32)
        high, low, seen = (part[:, :128] + part[:, 128:] for part in jnp.split(out, 3, axis=0))
        return high + low - jnp.where(left_half(seen.shape), seen, 0.0)

    def updated(own, total):
        return own - STEP_CAP * jnp.tanh((total / (swap(total) + EPSILON)) / STEP_CAP)

    def factor_step(it):
        def chunk(j, carry):
            there = (x + far_first(j)) % X
            out = sums(u_eta, v_eta, v_sum, cnt, there * UCHUNK, UCHUNK)
            part_u[it, there] = out.reshape(YH, CO, UROWS, 128)
            send(it, U_CORE + j, part_u.at[it, there, :, 1 - co], core_in.at[it, j], gene_dev(0, 0, 1))
            return carry

        lax.fori_loop(0, X, chunk, 0)
        for j, dx in enumerate(FAR_FIRST):
            there = (x + dx) % X
            started.append((it, U_CORE + j, core_in.at[it, j]))
            arrived(it, U_CORE + j, core_in.at[it, j])
            sum_u[it, j] = part_u[it, there, :, co] + core_in[it, j]
            for dh in (1, 0):
                if dx or dh:
                    slot = dx * YH + dh
                    sent(it, U_CHIP + slot, sum_u.at[it, j, (yh + dh) % YH], chip_in.at[it, slot], gene_dev(dx, dh, 0))
        total = sum_u[it, len(FAR_FIRST) - 1, yh]
        for dx, dh in [(1, 0), (3, 0), (0, 1), (2, 0), (1, 1), (3, 1), (2, 1)]:
            slot = dx * YH + dh
            arrived(it, U_CHIP + slot, chip_in.at[it, slot])
            total = total + chip_in[it, slot]
        own_u[...] = updated(own_u[...], total)

    def loading_step(it):
        def chunk(j, carry):
            there = (zg + far_first(j)) % ZG
            out = sums(v_eta, u_eta, u_sum, cnt_t, there * VCHUNK, VCHUNK)
            part_v[it, there] = out.reshape(ZL, YL, VROWS, 128)
            for d in (2, 3, 1, 0):
                send(it, V_PAIR + j * ZL + d, part_v.at[it, there, (zl + d) % ZL, 1 - yl], pair_in.at[it, j, d], cell_dev(0, 0, 1))
            return carry

        lax.fori_loop(0, ZG, chunk, 0)
        for j, dg in enumerate(FAR_FIRST):
            there = (zg + dg) % ZG
            for d in (2, 3, 1, 0):
                started.append((it, V_PAIR + j * ZL + d, pair_in.at[it, j, d]))
                arrived(it, V_PAIR + j * ZL + d, pair_in.at[it, j, d])
                sum1[it, j, d] = part_v[it, there, (zl + d) % ZL, yl] + pair_in[it, j, d]
                if d:
                    sent(it, V_LINE + j * ZL + d, sum1.at[it, j, d], line_in.at[it, j, d], cell_dev(0, d, 0))
        pending = take()
        for j, dg in enumerate(FAR_FIRST):
            total = sum1[it, j, 0]
            for d in (1, 2, 3):
                arrived(it, V_LINE + j * ZL + d, line_in.at[it, j, d])
                total = total + line_in[it, j, d]
            if dg:
                sum2[it, j] = total
                sent(it, V_RING + dg, sum2.at[it, j], ring_in.at[it, dg], cell_dev(dg, 0, 0))
        drain(pending)
        for dg in (1, 3, 2):
            arrived(it, V_RING + dg, ring_in.at[it, dg])
            total = total + ring_in[it, dg]
        own_v[...] = updated(own_v[...], total)

    gather_v_start(0)
    gather_u_start(0)
    offset_columns(cell_ref[...] * LOG2E, RANK, RANK + 3, cell_cols)
    offset_columns(gene_ref[...] * LOG2E, RANK + 3, RANK, gene_cols)

    def prepare(k, carry):
        load(k).wait()
        rows = pl.ds(pl.multiple_of(k * 256, 256), 256)
        block = cnt32[rows, :].astype(F32)
        cnt[rows, :] = block.astype(BF16)
        cnt_t[:, rows] = block.T.astype(BF16)
        return carry

    lax.fori_loop(0, CELLS // 256, prepare, 0)
    gather_u_forward(0)
    gather_v_forward(0)
    gather_u_finish(0)
    gather_v_finish(0)
    for it in range(ITERS):
        factor_step(it)
        pending = take()
        ubuf[it + 1, x, yh, co] = pack(own_u[...])
        gather_u_start(it + 1)
        if it + 1 == ITERS:
            new_rows[:UROWS] = own_u[...]
        drain(pending)
        gather_u_forward(it + 1)
        gather_u_finish(it + 1)
        loading_step(it)
        if it + 1 < ITERS:
            pending = take()
            vbuf[it + 1, z, yl] = pack(own_v[...])
            gather_v_start(it + 1)
            drain(pending)
            gather_v_forward(it + 1)
            gather_v_finish(it + 1)
    new_rows[UROWS:] = own_v[...]
    drain(take())


def per_device(counts, factors, loadings, cell_offset, gene_offset):
    arrays = (counts, factors, loadings, cell_offset.reshape(1, -1), gene_offset.reshape(1, -1))
    vmem = pl.BlockSpec(memory_space=pltpu.VMEM)
    hbm = pl.BlockSpec(memory_space=pltpu.HBM)
    scratch = [
        pltpu.VMEM((UROWS, RANK), F32),
        pltpu.VMEM((VROWS, RANK), F32),
        pltpu.VMEM((1, CELLS), F32),
        pltpu.VMEM((1, GENES), F32),
        pltpu.VMEM((CELLS, GENES), jnp.int32),
        pltpu.VMEM((CELLS, GENES), BF16),
        pltpu.VMEM((GENES, CELLS), BF16),
        pltpu.VMEM((CELLS, 256), BF16),
        pltpu.VMEM((CELLS, 256), BF16),
        pltpu.VMEM((GENES, 256), BF16),
        pltpu.VMEM((GENES, 256), BF16),
        pltpu.VMEM((CELLS, 128), F32),
        pltpu.VMEM((GENES, 128), F32),
        pltpu.VMEM((UROWS, 128), F32),
        pltpu.VMEM((VROWS, 128), F32),
        pltpu.VMEM((ITERS + 1, X, YH, CO, UROWS // 2, 128), F32),
        pltpu.VMEM((ITERS, Z, YL, VROWS // 2, 128), F32),
        pltpu.VMEM((ITERS, X, YH, CO, UROWS, 128), F32),
        pltpu.VMEM((ITERS, X, YH, UROWS, 128), F32),
        pltpu.VMEM((ITERS, X, YH, UROWS, 128), F32),
        pltpu.VMEM((ITERS, X * YH, UROWS, 128), F32),
        pltpu.VMEM((ITERS, ZG, ZL, YL, VROWS, 128), F32),
        pltpu.VMEM((ITERS, ZG, ZL, VROWS, 128), F32),
        pltpu.VMEM((ITERS, ZG, ZL, VROWS, 128), F32),
        pltpu.VMEM((ITERS, ZG, ZL, VROWS, 128), F32),
        pltpu.VMEM((ITERS, ZG, VROWS, 128), F32),
        pltpu.VMEM((ITERS, ZG, VROWS, 128), F32),
        pltpu.SemaphoreType.DMA((CELLS // 256 + 4,)),
        pltpu.SemaphoreType.DMA((ITERS + 1, SLOTS)),
        pltpu.SemaphoreType.DMA((ITERS + 1, SLOTS)),
    ]
    rows = pl.pallas_call(
        kernel,
        name="sweeps",
        out_shape=jax.ShapeDtypeStruct((UROWS + VROWS, 128), F32),
        in_specs=[hbm] * 5,
        out_specs=vmem,
        scratch_shapes=scratch,
        compiler_params=pltpu.CompilerParams(
            collective_id=0, has_side_effects=True, vmem_limit_bytes=48 * 1024 * 1024
        ),
    )(*(pltpu.with_memory_space_constraint(a, pltpu.HBM) for a in arrays))
    return rows[:UROWS, :RANK], rows[UROWS:, :RANK]


def solution(mesh):
    in_specs = (
        P("cell", "gene"),
        P(("cell", "gene"), None),
        P(("gene", "cell"), None),
        P("cell"),
        P("gene"),
    )
    out_specs = (P(("cell", "gene"), None), P(("gene", "cell"), None))
    return jax.shard_map(
        per_device, mesh=mesh, in_specs=in_specs, out_specs=out_specs, check_vma=False
    )
```

```python
import functools

import jax
import jax.numpy as jnp
from jax import lax
from jax.experimental import pallas as pl
from jax.experimental.pallas import tpu as pltpu
from jax.sharding import PartitionSpec as P

ITERS = 2
EPSILON = 1e-06
STEP_CAP = 0.25
LOG2E = 1.4426950408889634
F32, BF16 = jnp.float32, jnp.bfloat16
MESH = pl.DeviceIdType.MESH

ZG, ZL, YL = 4, 4, 2
Z = ZG * ZL
X, YH, CO = 4, 2, 2
RANK = 64
UROWS, VROWS = 64, 32
CELLS = X * YH * CO * UROWS
GENES = ZG * ZL * YL * VROWS
UCHUNK = YH * CO * UROWS
VCHUNK = ZL * YL * VROWS
FAR_FIRST = (2, 1, 3, 0)
SHIFT = 2
ZROWS = YL * VROWS
TILE = 256
U_CORE = 0
U_CHIP = U_CORE + X
V_PAIR = U_CHIP + X * YH
V_LINE = V_PAIR + ZG * ZL
V_RING = V_LINE + ZG * ZL
GU_CHIP = V_RING + ZG
GU_CORE = GU_CHIP + X * YH
GV_Z = GU_CORE + X * YH
GV_PAIR = GV_Z + ZG * ZL
SLOTS = GV_PAIR + ZG * ZL


def split(x):
    high = x.astype(BF16).astype(F32)
    return high, x - high


def left_half(shape):
    return lax.broadcasted_iota(jnp.int32, shape, len(shape) - 1) < RANK


def swap(x):
    return pltpu.roll(x, RANK, axis=x.ndim - 1)


def pairs(left, right):
    mask = left_half(left.shape)
    first = jnp.where(mask, left, swap(right))
    second = jnp.where(mask, swap(left), right)
    return first, second


def near_first(t):
    return t + t // 2 - 2 * (t // 3)


def far_first(j):
    return (2 + 3 * j - (j * (j - 1)) // 2) % 4


def kernel(
    counts_hbm, u_hbm, v_hbm, cell_hbm, gene_hbm, new_rows,
    u_ref, v_ref, cell_ref, gene_ref, cnt32, cnt, cnt_t, u_eta, u_sum, v_eta, v_sum, cell_cols, gene_cols,
    own_u, own_v, ubuf, vbuf, part_u, core_in, sum_u, chip_in,
    part_v, pair_in, sum1, line_in, sum2, ring_in, load_sem, send_sem, recv_sem,
):
    c, g = lax.axis_index("cell"), lax.axis_index("gene")
    chip, co = g // CO, g % CO
    x, yh = chip // YH, chip % YH
    shift = SHIFT * co
    z, yl = (c // YL + shift) % Z, c % YL
    zg, zl = z // ZL, z % ZL
    turn = shift * ZROWS

    def cell_dev(dg, dl, dy):
        there = ((zg + dg) % ZG) * ZL + (zl + dl) % ZL
        return (((there - shift + Z) % Z) * YL + (yl + dy) % YL, g)

    def gene_dev(dx, dh, dc):
        there = ((x + dx) % X) * YH + (yh + dh) % YH
        return (c, there * CO + (co + dc) % CO)

    def z_dev(d):
        return (((z + d - shift + Z) % Z) * YL + yl, g)

    far = [d for k in range(Z // 2, 0, -1) for d in dict.fromkeys((k, Z - k))]
    chips = [(dx, dh) for dx in FAR_FIRST for dh in (1, 0) if dx or dh]
    peers = [z_dev(d) for d in far] + [gene_dev(dx, dh, 0) for dx, dh in chips]
    peers += [cell_dev(0, 0, 1), gene_dev(0, 0, 1)]
    def load(k):
        rows = pl.ds(k * 256, 256)
        return pltpu.make_async_copy(counts_hbm.at[rows], cnt32.at[rows], load_sem.at[k])

    small = [
        pltpu.make_async_copy(src, dst, load_sem.at[CELLS // 256 + k])
        for k, (src, dst) in enumerate(
            ((v_hbm, v_ref), (u_hbm, u_ref), (cell_hbm, cell_ref), (gene_hbm, gene_ref))
        )
    ]
    for copy in small:
        copy.start()
    for k in range(CELLS // 256):
        load(k).start()

    barrier = pltpu.get_barrier_semaphore()
    for peer in peers:
        pl.semaphore_signal(barrier, inc=1, device_id=peer, device_id_type=MESH)

    started = []

    def send(era, slot, src, dst, device):
        copy = pltpu.make_async_remote_copy(
            src_ref=src, dst_ref=dst, send_sem=send_sem.at[era, slot],
            recv_sem=recv_sem.at[era, slot], device_id=device, device_id_type=MESH,
        )
        copy.start()

    def sent(era, slot, src, dst, device):
        send(era, slot, src, dst, device)
        started.append((era, slot, src))

    def take():
        pending = list(started)
        started.clear()
        return pending

    def drain(pending):
        for era, slot, src in pending:
            pltpu.make_async_remote_copy(
                src_ref=src, dst_ref=src, send_sem=send_sem.at[era, slot],
                recv_sem=recv_sem.at[era, slot], device_id=(c, g), device_id_type=MESH,
            ).wait_send()

    def arrived(era, slot, ref):
        pltpu.make_async_remote_copy(
            src_ref=ref, dst_ref=ref, send_sem=send_sem.at[era, slot],
            recv_sem=recv_sem.at[era, slot], device_id=(c, g), device_id_type=MESH,
        ).wait_recv()

    def pack(rows):
        half = rows.shape[0] // 2
        return jnp.where(left_half((half, 128)), rows[:half], swap(rows[half:]))

    own_u[...] = jnp.zeros_like(own_u)
    own_v[...] = jnp.zeros_like(own_v)
    for copy in small:
        copy.wait()
    own_u[:, :RANK] = u_ref[...]
    own_v[:, :RANK] = v_ref[...]

    def offset_columns(row, first_offset, first_one, turn, out):
        high, rest = split(row)
        mid, low = split(rest)
        index = lax.broadcasted_iota(jnp.int32, (128, row.shape[1]), 0)
        rows = jnp.zeros((128, row.shape[1]), F32)
        for k, part in enumerate((high, mid, low)):
            rows = jnp.where(index == first_offset + k, part, rows)
            rows = jnp.where(index == first_one + k, 1.0, rows)
        out[...] = (rows if turn is None else pltpu.roll(rows, turn, axis=1)).T

    ubuf[0, x, yh, co] = pack(own_u[...])
    vbuf[0, z, yl] = pack(own_v[...])
    pl.semaphore_wait(barrier, len(peers))

    def gather_u_start(era):
        mine = ubuf.at[era, x, yh, co]
        for dx, dh in chips:
            sent(era, GU_CHIP + dx * YH + dh, mine, mine, gene_dev(dx, dh, 0))
        sent(era, GU_CORE, mine, mine, gene_dev(0, 0, 1))

    def gather_u_forward(era):
        for dx, dh in [(1, 0), (3, 0), (0, 1), (2, 0), (1, 1), (3, 1), (2, 1)]:
            block = ubuf.at[era, (x - dx) % X, (yh - dh) % YH, co]
            arrived(era, GU_CHIP + dx * YH + dh, block)
            sent(era, GU_CORE + dx * YH + dh, block, block, gene_dev(0, 0, 1))

    def gather_u_finish(era):
        def tile(t, carry):
            dx = near_first(t)
            there = (x - dx + X) % X
            for dh in range(YH):
                arrived(era, GU_CORE + dx * YH + dh, ubuf.at[era, there, (yh - dh) % YH, 1 - co])
            packed = ubuf[era, there].reshape(YH * CO, UROWS // 2, 128)
            assemble(packed, there * TILE, u_eta, u_sum, cell_cols, True)
            return carry

        lax.fori_loop(0, X, tile, 0)

    def gather_v_start(era):
        mine = vbuf.at[era, z, yl]
        for d in far:
            sent(era, GV_Z + d, mine, mine, z_dev(d))
        sent(era, GV_PAIR, mine, mine, cell_dev(0, 0, 1))

    def gather_v_forward(era):
        for d in reversed(far):
            block = vbuf.at[era, (z - d) % Z, yl]
            arrived(era, GV_Z + d, block)
            sent(era, GV_PAIR + d, block, block, cell_dev(0, 0, 1))

    def gather_v_finish(era):
        def tile(t, carry):
            there = (zg + near_first(t)) % ZG
            for k in range(ZL):
                source = there * ZL + k
                arrived(era, GV_PAIR + (z - source + Z) % Z, vbuf.at[era, source, 1 - yl])
            packed = vbuf[era, pl.ds(there * ZL, ZL)].reshape(ZL * YL, VROWS // 2, 128)
            assemble(packed, there * TILE, v_eta, v_sum, gene_cols, False)
            return carry

        lax.fori_loop(0, ZG, tile, 0)

    def assemble(packed, first_row, eta, total, columns, scale):
        rows = pl.ds(pl.multiple_of(first_row, TILE), TILE)
        plain_h, plain_l = split(packed)
        square_h, square_l = split(packed * packed)

        def put(ref, column, left, right):
            both = jnp.concatenate([half.astype(BF16) for half in pairs(left, right)], axis=1)
            ref[rows, column:column + 128] = both.reshape(TILE, 128)

        put(total, 0, plain_h, square_h)
        put(total, 128, plain_l, square_l)
        if scale:
            high, low = split(packed * LOG2E)
            put(eta, 0, high, low)
            third = high
        else:
            put(eta, 0, plain_h, plain_h)
            third = plain_l
        both = jnp.concatenate(pairs(third, third), axis=1).reshape(TILE, 128)
        eta[rows, 128:] = jnp.where(left_half(both.shape), both, columns[rows, :]).astype(BF16)

    def sums(row_eta, column_eta, weights, count_ref, first, rows):
        here = pl.ds(pl.multiple_of(first, rows), rows)
        eta = lax.dot_general(
            row_eta[here, :], column_eta[...], (((1,), (1,)), ((), ())), preferred_element_type=F32
        )
        means = jnp.exp2(eta)
        high = means.astype(BF16)
        low = (means - high.astype(F32)).astype(BF16)
        stacked = jnp.concatenate([high, low, count_ref[here, :]], axis=0)
        out = jnp.dot(stacked, weights[...], preferred_element_type=F32)
        high, low, seen = (part[:, :128] + part[:, 128:] for part in jnp.split(out, 3, axis=0))
        return high + low - jnp.where(left_half(seen.shape), seen, 0.0)

    def updated(own, total):
        return own - STEP_CAP * jnp.tanh((total / (swap(total) + EPSILON)) / STEP_CAP)

    def factor_step(it):
        def serve(j, steps):
            dx = far_first(j)
            arrived(it, U_CORE + j, core_in.at[it, j])
            sum_u[it, j] = part_u[it, (x + dx) % X, :, co] + core_in[it, j]
            for dh in steps:
                slot = dx * YH + dh
                send(it, U_CHIP + slot, sum_u.at[it, j, (yh + dh) % YH], chip_in.at[it, slot], gene_dev(dx, dh, 0))

        def chunk(j, carry):
            there = (x + far_first(j)) % X
            out = sums(u_eta, v_eta, v_sum, cnt, there * UCHUNK, UCHUNK)
            part_u[it, there] = out.reshape(YH, CO, UROWS, 128)
            send(it, U_CORE + j, part_u.at[it, there, :, 1 - co], core_in.at[it, j], gene_dev(0, 0, 1))

            @pl.when(j > 0)
            def _():
                serve(j - 1, (1, 0))

            return carry

        lax.fori_loop(0, X, chunk, 0)
        serve(X - 1, (1,))
        started.extend((it, U_CORE + j, core_in.at[it, j]) for j in range(X))
        started.extend((it, U_CHIP + slot, chip_in.at[it, slot]) for slot in range(1, X * YH))
        total = sum_u[it, len(FAR_FIRST) - 1, yh]
        for dx, dh in [(1, 0), (3, 0), (0, 1), (2, 0), (1, 1), (3, 1), (2, 1)]:
            slot = dx * YH + dh
            arrived(it, U_CHIP + slot, chip_in.at[it, slot])
            total = total + chip_in[it, slot]
        own_u[...] = updated(own_u[...], total)

    def loading_step(it):
        def chunk(j, carry):
            there = (zg + far_first(j)) % ZG
            out = sums(v_eta, u_eta, u_sum, cnt_t, there * VCHUNK, VCHUNK)
            part_v[it, there] = out.reshape(ZL, YL, VROWS, 128)
            for d in (2, 3, 1, 0):
                send(it, V_PAIR + j * ZL + d, part_v.at[it, there, (zl + d) % ZL, 1 - yl], pair_in.at[it, j, d], cell_dev(0, 0, 1))
            return carry

        lax.fori_loop(0, ZG, chunk, 0)
        for j, dg in enumerate(FAR_FIRST):
            there = (zg + dg) % ZG
            for d in (2, 3, 1, 0):
                started.append((it, V_PAIR + j * ZL + d, pair_in.at[it, j, d]))
                arrived(it, V_PAIR + j * ZL + d, pair_in.at[it, j, d])
                sum1[it, j, d] = part_v[it, there, (zl + d) % ZL, yl] + pair_in[it, j, d]
                if d:
                    sent(it, V_LINE + j * ZL + d, sum1.at[it, j, d], line_in.at[it, j, d], cell_dev(0, d, 0))
        pending = take()
        for j, dg in enumerate(FAR_FIRST):
            total = sum1[it, j, 0]
            for d in (1, 2, 3):
                arrived(it, V_LINE + j * ZL + d, line_in.at[it, j, d])
                total = total + line_in[it, j, d]
            if dg:
                sum2[it, j] = total
                sent(it, V_RING + dg, sum2.at[it, j], ring_in.at[it, dg], cell_dev(dg, 0, 0))
        drain(pending)
        for dg in (1, 3, 2):
            arrived(it, V_RING + dg, ring_in.at[it, dg])
            total = total + ring_in[it, dg]
        own_v[...] = updated(own_v[...], total)

    gather_v_start(0)
    gather_u_start(0)
    offset_columns(cell_ref[...] * LOG2E, RANK, RANK + 3, None, cell_cols)
    offset_columns(gene_ref[...] * LOG2E, RANK + 3, RANK, turn, gene_cols)

    def prepare(k, carry):
        load(k).wait()
        rows = pl.ds(pl.multiple_of(k * 256, 256), 256)
        block = pltpu.roll(cnt32[rows, :].astype(F32), turn, axis=1)
        cnt[rows, :] = block.astype(BF16)
        cnt_t[:, rows] = block.T.astype(BF16)
        return carry

    lax.fori_loop(0, CELLS // 256, prepare, 0)
    gather_u_forward(0)
    gather_v_forward(0)
    gather_u_finish(0)
    gather_v_finish(0)
    for it in range(ITERS):
        factor_step(it)
        pending = take()
        ubuf[it + 1, x, yh, co] = pack(own_u[...])
        gather_u_start(it + 1)
        if it + 1 == ITERS:
            new_rows[:UROWS] = own_u[...]
        drain(pending)
        gather_u_forward(it + 1)
        gather_u_finish(it + 1)
        loading_step(it)
        if it + 1 < ITERS:
            pending = take()
            vbuf[it + 1, z, yl] = pack(own_v[...])
            gather_v_start(it + 1)
            drain(pending)
            gather_v_forward(it + 1)
            gather_v_finish(it + 1)
    new_rows[UROWS:] = own_v[...]
    drain(take())


def per_device(counts, factors, loadings, cell_offset, gene_offset):
    arrays = (counts, factors, loadings, cell_offset.reshape(1, -1), gene_offset.reshape(1, -1))
    vmem = pl.BlockSpec(memory_space=pltpu.VMEM)
    hbm = pl.BlockSpec(memory_space=pltpu.HBM)
    scratch = [
        pltpu.VMEM((UROWS, RANK), F32),
        pltpu.VMEM((VROWS, RANK), F32),
        pltpu.VMEM((1, CELLS), F32),
        pltpu.VMEM((1, GENES), F32),
        pltpu.VMEM((CELLS, GENES), jnp.int32),
        pltpu.VMEM((CELLS, GENES), BF16),
        pltpu.VMEM((GENES, CELLS), BF16),
        pltpu.VMEM((CELLS, 256), BF16),
        pltpu.VMEM((CELLS, 256), BF16),
        pltpu.VMEM((GENES, 256), BF16),
        pltpu.VMEM((GENES, 256), BF16),
        pltpu.VMEM((CELLS, 128), F32),
        pltpu.VMEM((GENES, 128), F32),
        pltpu.VMEM((UROWS, 128), F32),
        pltpu.VMEM((VROWS, 128), F32),
        pltpu.VMEM((ITERS + 1, X, YH, CO, UROWS // 2, 128), F32),
        pltpu.VMEM((ITERS, Z, YL, VROWS // 2, 128), F32),
        pltpu.VMEM((ITERS, X, YH, CO, UROWS, 128), F32),
        pltpu.VMEM((ITERS, X, YH, UROWS, 128), F32),
        pltpu.VMEM((ITERS, X, YH, UROWS, 128), F32),
        pltpu.VMEM((ITERS, X * YH, UROWS, 128), F32),
        pltpu.VMEM((ITERS, ZG, ZL, YL, VROWS, 128), F32),
        pltpu.VMEM((ITERS, ZG, ZL, VROWS, 128), F32),
        pltpu.VMEM((ITERS, ZG, ZL, VROWS, 128), F32),
        pltpu.VMEM((ITERS, ZG, ZL, VROWS, 128), F32),
        pltpu.VMEM((ITERS, ZG, VROWS, 128), F32),
        pltpu.VMEM((ITERS, ZG, VROWS, 128), F32),
        pltpu.SemaphoreType.DMA((CELLS // 256 + 4,)),
        pltpu.SemaphoreType.DMA((ITERS + 1, SLOTS)),
        pltpu.SemaphoreType.DMA((ITERS + 1, SLOTS)),
    ]
    rows = pl.pallas_call(
        kernel,
        name="sweeps",
        out_shape=jax.ShapeDtypeStruct((UROWS + VROWS, 128), F32),
        in_specs=[hbm] * 5,
        out_specs=vmem,
        scratch_shapes=scratch,
        compiler_params=pltpu.CompilerParams(
            collective_id=0, has_side_effects=True, vmem_limit_bytes=48 * 1024 * 1024
        ),
    )(*(pltpu.with_memory_space_constraint(a, pltpu.HBM) for a in arrays))
    return rows[:UROWS, :RANK], rows[UROWS:, :RANK]


def solution(mesh):
    in_specs = (
        P("cell", "gene"),
        P(("cell", "gene"), None),
        P(("gene", "cell"), None),
        P("cell"),
        P("gene"),
    )
    out_specs = (P(("cell", "gene"), None), P(("gene", "cell"), None))
    return jax.shard_map(
        per_device, mesh=mesh, in_specs=in_specs, out_specs=out_specs, check_vma=False
    )
```

```python
import functools

import jax
import jax.numpy as jnp
from jax import lax
from jax.experimental import pallas as pl
from jax.experimental.pallas import tpu as pltpu
from jax.sharding import PartitionSpec as P

ITERS = 2
EPSILON = 1e-06
STEP_CAP = 0.25
LOG2E = 1.4426950408889634
F32, BF16 = jnp.float32, jnp.bfloat16
MESH = pl.DeviceIdType.MESH

ZG, ZL, YL = 4, 4, 2
Z = ZG * ZL
X, YH, CO = 4, 2, 2
RANK = 64
UROWS, VROWS = 64, 32
CELLS = X * YH * CO * UROWS
GENES = ZG * ZL * YL * VROWS
UCHUNK = YH * CO * UROWS
VCHUNK = ZL * YL * VROWS
FAR_FIRST = (2, 1, 3, 0)
SHIFT = 2
REACH = Z // 4
ZROWS = YL * VROWS
TILE = 256
U_CORE = 0
U_CHIP = U_CORE + X
V_PAIR = U_CHIP + X * YH
V_LINE = V_PAIR + ZG * ZL
V_RING = V_LINE + ZG * ZL
GU_CHIP = V_RING + ZG
GU_CORE = GU_CHIP + X * YH
GV_Z = GU_CORE + X * YH
GV_PAIR = GV_Z + ZG * ZL
SLOTS = GV_PAIR + ZG * ZL


def split(x):
    high = x.astype(BF16).astype(F32)
    return high, x - high


def left_half(shape):
    return lax.broadcasted_iota(jnp.int32, shape, len(shape) - 1) < RANK


def swap(x):
    return pltpu.roll(x, RANK, axis=x.ndim - 1)


def pairs(left, right):
    mask = left_half(left.shape)
    first = jnp.where(mask, left, swap(right))
    second = jnp.where(mask, swap(left), right)
    return first, second


def near_first(t):
    return t + t // 2 - 2 * (t // 3)


def far_first(j):
    return (2 + 3 * j - (j * (j - 1)) // 2) % 4


def kernel(
    counts_hbm, u_hbm, v_hbm, cell_hbm, gene_hbm, new_rows,
    u_ref, v_ref, cell_ref, gene_ref, cnt32, cnt, cnt_t, u_eta, u_sum, v_eta, v_sum, cell_cols, gene_cols,
    own_u, own_v, ubuf, vbuf, part_u, core_in, sum_u, chip_in,
    part_v, pair_in, sum1, line_in, sum2, ring_in, load_sem, send_sem, recv_sem,
):
    c, g = lax.axis_index("cell"), lax.axis_index("gene")
    chip, co = g // CO, g % CO
    x, yh = chip // YH, chip % YH
    shift = SHIFT * co
    z, yl = (c // YL + shift) % Z, c % YL
    zg, zl = z // ZL, z % ZL
    turn = shift * ZROWS

    def cell_dev(dg, dl, dy):
        there = ((zg + dg) % ZG) * ZL + (zl + dl) % ZL
        return (((there - shift + Z) % Z) * YL + (yl + dy) % YL, g)

    def gene_dev(dx, dh, dc):
        there = ((x + dx) % X) * YH + (yh + dh) % YH
        return (c, there * CO + (co + dc) % CO)

    def z_dev(d):
        return (((z + d - shift + Z) % Z) * YL + yl, g)

    far = [d for k in range(Z // 2, 0, -1) for d in dict.fromkeys((k, Z - k))]
    chips = [(dx, dh) for dx in FAR_FIRST for dh in (1, 0) if dx or dh]
    near = [d for d in far if min(d, Z - d) <= REACH]
    peers = [z_dev(d) for d in near] + [gene_dev(dx, dh, 0) for dx, dh in chips]
    peers += [cell_dev(0, 0, 1), gene_dev(0, 0, 1)]
    def load(k):
        rows = pl.ds(k * 256, 256)
        return pltpu.make_async_copy(counts_hbm.at[rows], cnt32.at[rows], load_sem.at[k])

    small = [
        pltpu.make_async_copy(src, dst, load_sem.at[CELLS // 256 + k])
        for k, (src, dst) in enumerate(
            ((v_hbm, v_ref), (u_hbm, u_ref), (cell_hbm, cell_ref), (gene_hbm, gene_ref))
        )
    ]
    for copy in small:
        copy.start()
    for k in range(CELLS // 256):
        load(k).start()

    barrier = pltpu.get_barrier_semaphore()
    for peer in peers:
        pl.semaphore_signal(barrier, inc=1, device_id=peer, device_id_type=MESH)

    started = []

    def send(era, slot, src, dst, device):
        copy = pltpu.make_async_remote_copy(
            src_ref=src, dst_ref=dst, send_sem=send_sem.at[era, slot],
            recv_sem=recv_sem.at[era, slot], device_id=device, device_id_type=MESH,
        )
        copy.start()

    def sent(era, slot, src, dst, device):
        send(era, slot, src, dst, device)
        started.append((era, slot, src))

    def take():
        pending = list(started)
        started.clear()
        return pending

    def drain(pending):
        for era, slot, src in pending:
            pltpu.make_async_remote_copy(
                src_ref=src, dst_ref=src, send_sem=send_sem.at[era, slot],
                recv_sem=recv_sem.at[era, slot], device_id=(c, g), device_id_type=MESH,
            ).wait_send()

    def arrived(era, slot, ref):
        pltpu.make_async_remote_copy(
            src_ref=ref, dst_ref=ref, send_sem=send_sem.at[era, slot],
            recv_sem=recv_sem.at[era, slot], device_id=(c, g), device_id_type=MESH,
        ).wait_recv()

    def pack(rows):
        half = rows.shape[0] // 2
        return jnp.where(left_half((half, 128)), rows[:half], swap(rows[half:]))

    own_u[...] = jnp.zeros_like(own_u)
    own_v[...] = jnp.zeros_like(own_v)
    for copy in small:
        copy.wait()
    own_u[:, :RANK] = u_ref[...]
    own_v[:, :RANK] = v_ref[...]

    def offset_columns(row, first_offset, first_one, turn, out):
        high, rest = split(row)
        mid, low = split(rest)
        index = lax.broadcasted_iota(jnp.int32, (128, row.shape[1]), 0)
        rows = jnp.zeros((128, row.shape[1]), F32)
        for k, part in enumerate((high, mid, low)):
            rows = jnp.where(index == first_offset + k, part, rows)
            rows = jnp.where(index == first_one + k, 1.0, rows)
        out[...] = (rows if turn is None else pltpu.roll(rows, turn, axis=1)).T

    ubuf[0, x, yh, co] = pack(own_u[...])
    vbuf[0, z, yl] = pack(own_v[...])
    pl.semaphore_wait(barrier, len(peers))

    def gather_u_start(era):
        mine = ubuf.at[era, x, yh, co]
        for dx, dh in chips:
            sent(era, GU_CHIP + dx * YH + dh, mine, mine, gene_dev(dx, dh, 0))
        sent(era, GU_CORE, mine, mine, gene_dev(0, 0, 1))

    def gather_u_forward(era):
        for dx, dh in [(1, 0), (3, 0), (0, 1), (2, 0), (1, 1), (3, 1), (2, 1)]:
            block = ubuf.at[era, (x - dx) % X, (yh - dh) % YH, co]
            arrived(era, GU_CHIP + dx * YH + dh, block)
            sent(era, GU_CORE + dx * YH + dh, block, block, gene_dev(0, 0, 1))

    def gather_u_finish(era):
        def tile(t, carry):
            dx = near_first(t)
            there = (x - dx + X) % X
            for dh in range(YH):
                arrived(era, GU_CORE + dx * YH + dh, ubuf.at[era, there, (yh - dh) % YH, 1 - co])
            packed = ubuf[era, there].reshape(YH * CO, UROWS // 2, 128)
            assemble(packed, there * TILE, u_eta, u_sum, cell_cols, True)
            return carry

        lax.fori_loop(0, X, tile, 0)

    def gather_v_start(era):
        mine = vbuf.at[era, z, yl]
        for d in far if era else near:
            sent(era, GV_Z + d, mine, mine, z_dev(d))
        sent(era, GV_PAIR, mine, mine, cell_dev(0, 0, 1))

    def gather_v_forward(era):
        for d in list(reversed(far)) if era else near + list(reversed(far))[len(near):]:
            block = vbuf.at[era, (z - d + Z) % Z, yl]
            arrived(era, GV_Z + d, block)
            if not era and min(d, Z - d) == REACH:
                for k in range(REACH, 0, -1):
                    if d == REACH:
                        sent(era, GV_Z + d + k, block, block, z_dev(k))
                    elif d - k > Z // 2:
                        sent(era, GV_Z + d - k, block, block, z_dev(Z - k))
            sent(era, GV_PAIR + d, block, block, cell_dev(0, 0, 1))

    def gather_v_finish(era):
        def tile(t, carry):
            there = (zg + near_first(t)) % ZG
            for k in range(ZL):
                source = there * ZL + k
                arrived(era, GV_PAIR + (z - source + Z) % Z, vbuf.at[era, source, 1 - yl])
            packed = vbuf[era, pl.ds(there * ZL, ZL)].reshape(ZL * YL, VROWS // 2, 128)
            assemble(packed, there * TILE, v_eta, v_sum, gene_cols, False)
            return carry

        lax.fori_loop(0, ZG, tile, 0)

    def assemble(packed, first_row, eta, total, columns, scale):
        rows = pl.ds(pl.multiple_of(first_row, TILE), TILE)
        plain_h, plain_l = split(packed)
        square_h, square_l = split(packed * packed)

        def put(ref, column, left, right):
            both = jnp.concatenate([half.astype(BF16) for half in pairs(left, right)], axis=1)
            ref[rows, column:column + 128] = both.reshape(TILE, 128)

        put(total, 0, plain_h, square_h)
        put(total, 128, plain_l, square_l)
        if scale:
            high, low = split(packed * LOG2E)
            put(eta, 0, high, low)
            third = high
        else:
            put(eta, 0, plain_h, plain_h)
            third = plain_l
        both = jnp.concatenate(pairs(third, third), axis=1).reshape(TILE, 128)
        eta[rows, 128:] = jnp.where(left_half(both.shape), both, columns[rows, :]).astype(BF16)

    def sums(row_eta, column_eta, weights, count_ref, first, rows):
        here = pl.ds(pl.multiple_of(first, rows), rows)
        eta = lax.dot_general(
            row_eta[here, :], column_eta[...], (((1,), (1,)), ((), ())), preferred_element_type=F32
        )
        means = jnp.exp2(eta)
        high = means.astype(BF16)
        low = (means - high.astype(F32)).astype(BF16)
        stacked = jnp.concatenate([high, low, count_ref[here, :]], axis=0)
        out = jnp.dot(stacked, weights[...], preferred_element_type=F32)
        high, low, seen = (part[:, :128] + part[:, 128:] for part in jnp.split(out, 3, axis=0))
        return high + low - jnp.where(left_half(seen.shape), seen, 0.0)

    def updated(own, total):
        return own - STEP_CAP * jnp.tanh((total / (swap(total) + EPSILON)) / STEP_CAP)

    def factor_step(it):
        def serve(j, steps):
            dx = far_first(j)
            arrived(it, U_CORE + j, core_in.at[it, j])
            sum_u[it, j] = part_u[it, (x + dx) % X, :, co] + core_in[it, j]
            for dh in steps:
                slot = dx * YH + dh
                send(it, U_CHIP + slot, sum_u.at[it, j, (yh + dh) % YH], chip_in.at[it, slot], gene_dev(dx, dh, 0))

        def chunk(j, carry):
            there = (x + far_first(j)) % X
            out = sums(u_eta, v_eta, v_sum, cnt, there * UCHUNK, UCHUNK)
            part_u[it, there] = out.reshape(YH, CO, UROWS, 128)
            send(it, U_CORE + j, part_u.at[it, there, :, 1 - co], core_in.at[it, j], gene_dev(0, 0, 1))

            @pl.when(j > 0)
            def _():
                serve(j - 1, (1, 0))

            return carry

        lax.fori_loop(0, X, chunk, 0)
        serve(X - 1, (1,))
        started.extend((it, U_CORE + j, core_in.at[it, j]) for j in range(X))
        started.extend((it, U_CHIP + slot, chip_in.at[it, slot]) for slot in range(1, X * YH))
        total = sum_u[it, len(FAR_FIRST) - 1, yh]
        for dx, dh in [(1, 0), (3, 0), (0, 1), (2, 0), (1, 1), (3, 1), (2, 1)]:
            slot = dx * YH + dh
            arrived(it, U_CHIP + slot, chip_in.at[it, slot])
            total = total + chip_in[it, slot]
        own_u[...] = updated(own_u[...], total)

    def loading_step(it):
        def chunk(j, carry):
            there = (zg + far_first(j)) % ZG
            out = sums(v_eta, u_eta, u_sum, cnt_t, there * VCHUNK, VCHUNK)
            part_v[it, there] = out.reshape(ZL, YL, VROWS, 128)
            for d in (2, 3, 1, 0):
                send(it, V_PAIR + j * ZL + d, part_v.at[it, there, (zl + d) % ZL, 1 - yl], pair_in.at[it, j, d], cell_dev(0, 0, 1))
            return carry

        lax.fori_loop(0, ZG, chunk, 0)
        for j, dg in enumerate(FAR_FIRST):
            there = (zg + dg) % ZG
            for d in (2, 3, 1, 0):
                started.append((it, V_PAIR + j * ZL + d, pair_in.at[it, j, d]))
                arrived(it, V_PAIR + j * ZL + d, pair_in.at[it, j, d])
                sum1[it, j, d] = part_v[it, there, (zl + d) % ZL, yl] + pair_in[it, j, d]
                if d:
                    sent(it, V_LINE + j * ZL + d, sum1.at[it, j, d], line_in.at[it, j, d], cell_dev(0, d, 0))
        pending = take()
        for j, dg in enumerate(FAR_FIRST):
            total = sum1[it, j, 0]
            for d in (1, 2, 3):
                arrived(it, V_LINE + j * ZL + d, line_in.at[it, j, d])
                total = total + line_in[it, j, d]
            if dg:
                sum2[it, j] = total
                sent(it, V_RING + dg, sum2.at[it, j], ring_in.at[it, dg], cell_dev(dg, 0, 0))
        drain(pending)
        for dg in (1, 3, 2):
            arrived(it, V_RING + dg, ring_in.at[it, dg])
            total = total + ring_in[it, dg]
        own_v[...] = updated(own_v[...], total)

    gather_v_start(0)
    gather_u_start(0)
    offset_columns(cell_ref[...] * LOG2E, RANK, RANK + 3, None, cell_cols)
    offset_columns(gene_ref[...] * LOG2E, RANK + 3, RANK, turn, gene_cols)

    def prepare(k, carry):
        load(k).wait()
        rows = pl.ds(pl.multiple_of(k * 256, 256), 256)
        block = pltpu.roll(cnt32[rows, :].astype(F32), turn, axis=1)
        cnt[rows, :] = block.astype(BF16)
        cnt_t[:, rows] = block.T.astype(BF16)
        return carry

    lax.fori_loop(0, CELLS // 256, prepare, 0)
    gather_u_forward(0)
    gather_v_forward(0)
    gather_u_finish(0)
    gather_v_finish(0)
    for it in range(ITERS):
        factor_step(it)
        pending = take()
        ubuf[it + 1, x, yh, co] = pack(own_u[...])
        gather_u_start(it + 1)
        if it + 1 == ITERS:
            new_rows[:UROWS] = own_u[...]
        drain(pending)
        gather_u_forward(it + 1)
        gather_u_finish(it + 1)
        loading_step(it)
        if it + 1 < ITERS:
            pending = take()
            vbuf[it + 1, z, yl] = pack(own_v[...])
            gather_v_start(it + 1)
            drain(pending)
            gather_v_forward(it + 1)
            gather_v_finish(it + 1)
    new_rows[UROWS:] = own_v[...]
    drain(take())


def per_device(counts, factors, loadings, cell_offset, gene_offset):
    arrays = (counts, factors, loadings, cell_offset.reshape(1, -1), gene_offset.reshape(1, -1))
    vmem = pl.BlockSpec(memory_space=pltpu.VMEM)
    hbm = pl.BlockSpec(memory_space=pltpu.HBM)
    scratch = [
        pltpu.VMEM((UROWS, RANK), F32),
        pltpu.VMEM((VROWS, RANK), F32),
        pltpu.VMEM((1, CELLS), F32),
        pltpu.VMEM((1, GENES), F32),
        pltpu.VMEM((CELLS, GENES), jnp.int32),
        pltpu.VMEM((CELLS, GENES), BF16),
        pltpu.VMEM((GENES, CELLS), BF16),
        pltpu.VMEM((CELLS, 256), BF16),
        pltpu.VMEM((CELLS, 256), BF16),
        pltpu.VMEM((GENES, 256), BF16),
        pltpu.VMEM((GENES, 256), BF16),
        pltpu.VMEM((CELLS, 128), F32),
        pltpu.VMEM((GENES, 128), F32),
        pltpu.VMEM((UROWS, 128), F32),
        pltpu.VMEM((VROWS, 128), F32),
        pltpu.VMEM((ITERS + 1, X, YH, CO, UROWS // 2, 128), F32),
        pltpu.VMEM((ITERS, Z, YL, VROWS // 2, 128), F32),
        pltpu.VMEM((ITERS, X, YH, CO, UROWS, 128), F32),
        pltpu.VMEM((ITERS, X, YH, UROWS, 128), F32),
        pltpu.VMEM((ITERS, X, YH, UROWS, 128), F32),
        pltpu.VMEM((ITERS, X * YH, UROWS, 128), F32),
        pltpu.VMEM((ITERS, ZG, ZL, YL, VROWS, 128), F32),
        pltpu.VMEM((ITERS, ZG, ZL, VROWS, 128), F32),
        pltpu.VMEM((ITERS, ZG, ZL, VROWS, 128), F32),
        pltpu.VMEM((ITERS, ZG, ZL, VROWS, 128), F32),
        pltpu.VMEM((ITERS, ZG, VROWS, 128), F32),
        pltpu.VMEM((ITERS, ZG, VROWS, 128), F32),
        pltpu.SemaphoreType.DMA((CELLS // 256 + 4,)),
        pltpu.SemaphoreType.DMA((ITERS + 1, SLOTS)),
        pltpu.SemaphoreType.DMA((ITERS + 1, SLOTS)),
    ]
    rows = pl.pallas_call(
        kernel,
        name="sweeps",
        out_shape=jax.ShapeDtypeStruct((UROWS + VROWS, 128), F32),
        in_specs=[hbm] * 5,
        out_specs=vmem,
        scratch_shapes=scratch,
        compiler_params=pltpu.CompilerParams(
            collective_id=0, has_side_effects=True, vmem_limit_bytes=48 * 1024 * 1024
        ),
    )(*(pltpu.with_memory_space_constraint(a, pltpu.HBM) for a in arrays))
    return rows[:UROWS, :RANK], rows[UROWS:, :RANK]


def solution(mesh):
    in_specs = (
        P("cell", "gene"),
        P(("cell", "gene"), None),
        P(("gene", "cell"), None),
        P("cell"),
        P("gene"),
    )
    out_specs = (P(("cell", "gene"), None), P(("gene", "cell"), None))
    return jax.shard_map(
        per_device, mesh=mesh, in_specs=in_specs, out_specs=out_specs, check_vma=False
    )
```
